512 devices in a mesh: event: 64 (over z, x, core), wrow: 8 (over y).
Axes of the slice: x: 4, y: 8, z: 8, core: 2. Of those that a mesh axis runs over, the one named last changes fastest.
Arguments:
- mc_mass: float32 [196608], P('event'), may hold values from 0.5 to 4
- mc_basis: bfloat16 [64, 196608], P(None, 'event'), may hold values from -4 to 4
- data_mass: float32 [262144], P('event'), may hold values from 0.5 to 4
- data_basis: bfloat16 [64, 262144], P(None, 'event'), may hold values from -4 to 4
- data_weight: float32 [262144], P('event'), may hold values from 0.2 to 7.2, as said below
- res_mass: float32 [1024], P('wrow'), may hold values from 0.8 to 1.9
- res_width: float32 [1024], P('wrow'), may hold values from 0.05 to 0.5
- res_wave: int32 [1024], P('wrow'), may hold values from 0 to 511, as said below
- wave_q: int32 [512], P('wrow'), may hold values from 0 to 63
- couplings: float32 [2, 512], P(None, 'wrow'), may hold values from -0.25 to 0.25
Outputs:
- coupling_out: float32 [2, 512], P(None, 'wrow')
- intensity: float32 [262144], P('event')
The draws below stay inside these ranges and needn't reach their ends.
Inputs may be any that keep to these rules, and one draw needn't show every extreme that they name: Resonance r belongs to a wave of block r // 128: res_wave[r] // 64 == r // 128; every wave has exactly 2 resonances. `data_weight`: positive event weights.
All inputs are finite; a program needn't handle non-finite values.
Results may differ from the reference program's by a relative error of at most 0.0024.
Values may be sent and summed in bfloat16 or wider, within the bound.
No kernel may reach another device: no remote copies, remote signals or barrier semaphores. Data moves between devices by JAX's collectives and lax.ppermute only.
A program may use at most 64 MiB of HBM per device.

```python
import math
import jax
import jax.numpy as jnp
from jax import lax

W = 512
Q = 64
MC_DEV = 3072
DATA_DEV = 4096
ITERS = 3
RES = 1024
WAVE_DEV = 64
RES_DEV = 128
EVENTS_MC = 196608
EVENTS_DATA = 262144
N_EVENT = 64


def draw_res_wave(key, part):
    blocks = RES // RES_DEV
    subkeys = jax.random.split(key, blocks)
    pattern = jnp.arange(RES_DEV, dtype=jnp.int32) % WAVE_DEV
    local_wave = jax.vmap(lambda subkey: jax.random.permutation(subkey, pattern))(subkeys)
    offsets = (jnp.arange(blocks, dtype=jnp.int32) * WAVE_DEV)[:, None]
    return (local_wave + offsets).reshape(RES)


def draw_data_weight(key, part):
    position = jnp.arange(EVENTS_DATA, dtype=jnp.float32) / EVENTS_DATA
    spread = jax.random.uniform(key, (EVENTS_DATA,), jnp.float32, 0.5, 1.5)
    ramp = 1.0 + 2.0 * position
    return spread * ramp


def set_ends(drawn, key, smallest, top_value):
    shape = drawn.shape
    index_at = [jax.random.randint(jax.random.fold_in(key, axis), (), 0, shape[axis]) for axis in range(len(shape))]
    drawn = drawn.at[tuple(index_at)].set(smallest)
    longest = shape.index(max(shape))
    index_at[longest] = (index_at[longest] + 1) % shape[longest]
    return drawn.at[tuple(index_at)].set(top_value)


def level_of(own_key, shape, cuts, smallest, high):
    loudness = 1.0
    for dim, blocks in cuts:
        draws = jax.random.uniform(jax.random.fold_in(jax.random.fold_in(own_key, 6), dim), (blocks,), jnp.float32, smallest / len(cuts), high / len(cuts))
        loudness = loudness * jnp.repeat(jnp.exp(draws), shape[dim] // blocks).reshape((-1,) + (1,) * (len(shape) - 1 - dim))
    return loudness


def gaussian(own_key, extent, deviation, bound, pieces=(), kind=jnp.bfloat16):
    array = deviation * jax.random.normal(own_key, extent, jnp.float32)
    if pieces:
        array = array * level_of(own_key, extent, pieces, -0.22, 0.18)
    return jnp.clip(array, -bound, bound).astype(kind)


def setup_inputs(seed: int = 0) -> dict:
    key_of = jax.random.split(jax.random.key(seed), 11)
    return {
        "mc_mass": jnp.clip(0.5 + 3.5 * jax.random.uniform(key_of[0], (EVENTS_MC,), jnp.float32) ** level_of(key_of[0], (EVENTS_MC,), ((0, 64),), -0.2, 0.2), 0.5, 4.0),
        "mc_basis": gaussian(key_of[1], (Q, EVENTS_MC), 1.0, 4.0, ((1, 64),)),
        "data_mass": jnp.clip(0.5 + 3.5 * jax.random.uniform(key_of[2], (EVENTS_DATA,), jnp.float32) ** level_of(key_of[2], (EVENTS_DATA,), ((0, 64),), -0.2, 0.2), 0.5, 4.0),
        "data_basis": gaussian(key_of[3], (Q, EVENTS_DATA), 1.0, 4.0, ((1, 64),)),
        "data_weight": draw_data_weight(jax.random.fold_in(key_of[10], 71), 0),
        "res_mass": jnp.clip(0.8 + 1.09999996 * jax.random.uniform(key_of[5], (RES,), jnp.float32) ** level_of(key_of[5], (RES,), ((0, 8),), -0.2, 0.2), 0.8, 1.9),
        "res_width": jnp.clip(jnp.exp(math.log(0.5) - 2.3025851 * jax.random.uniform(key_of[6], (RES,), jnp.float32) ** level_of(key_of[6], (RES,), ((0, 8),), -0.2, 0.2)), 0.05, 0.5),
        "res_wave": draw_res_wave(jax.random.fold_in(key_of[10], 71), 0),
        "wave_q": set_ends(jax.random.randint(key_of[8], (W,), 0, Q), jax.random.fold_in(key_of[8], 1), 0, Q - 1).astype(jnp.int32),
        "couplings": gaussian(key_of[9], (2, W), W ** -0.5, 0.25, ((1, 8),), jnp.float32),
    }


BACKGROUND = 0.5


def amplitudes(mass_sq, angular_basis, res_mass, res_width, res_wave, wave_q):
    product = res_mass * res_width
    spacing = (res_mass * res_mass)[:, None] - mass_sq[None, :]
    denominator = spacing * spacing + (product * product)[:, None]
    real_part = product[:, None] * spacing / denominator
    imag_part = (product * product)[:, None] / denominator
    summed_real = jax.ops.segment_sum(real_part, res_wave, num_segments=W)
    summed_imag = jax.ops.segment_sum(imag_part, res_wave, num_segments=W)
    angular = angular_basis[wave_q, :].astype(jnp.float32)
    return jnp.concatenate([angular * summed_real, angular * summed_imag], axis=0).astype(jnp.bfloat16)


def reference(mc_mass, mc_basis, data_mass, data_basis, data_weight, res_mass, res_width, res_wave, wave_q, couplings):
    highest = lax.Precision.HIGHEST
    mc_blocks = (mc_mass.reshape(N_EVENT, MC_DEV), mc_basis.reshape(Q, N_EVENT, MC_DEV).transpose(1, 0, 2))

    def gram_step(running, block):
        stacked = amplitudes(block[0], block[1], res_mass, res_width, res_wave, wave_q)
        products = lax.dot_general(stacked, stacked, (((1,), (1,)), ((), ())), preferred_element_type=jnp.float32)
        return running + products, None

    products, unused = lax.scan(gram_step, jnp.zeros((2 * W, 2 * W), jnp.float32), mc_blocks)
    normalize = 1.0 / EVENTS_MC
    gram_real = (products[:W, :W] + products[W:, W:]) * normalize
    gram_imag = (products[:W, W:] - products[W:, :W]) * normalize
    row_weight = jnp.sum(jnp.abs(gram_real) + jnp.abs(gram_imag), axis=1)
    data_blocks = (data_mass.reshape(N_EVENT, DATA_DEV), data_basis.reshape(Q, N_EVENT, DATA_DEV).transpose(1, 0, 2), data_weight.reshape(N_EVENT, DATA_DEV))
    inverse_count = 1.0 / EVENTS_DATA

    def data_pass(coupling):
        kernel = jnp.stack([jnp.concatenate([coupling[0], -coupling[1]]), jnp.concatenate([coupling[1], coupling[0]])])

        def data_step(running, block):
            stacked = amplitudes(block[0], block[1], res_mass, res_width, res_wave, wave_q)
            field_sum = jnp.dot(kernel, stacked, preferred_element_type=jnp.float32, precision=highest)
            power = field_sum[0] * field_sum[0] + field_sum[1] * field_sum[1]
            intensity = power + BACKGROUND
            weighting = block[2] / intensity
            carried = jnp.stack([field_sum[0] * weighting, field_sum[1] * weighting], axis=1)
            projected = jnp.dot(stacked, carried, preferred_element_type=jnp.float32, precision=highest)
            real_amp = stacked[:W].astype(jnp.float32)
            imag_amp = stacked[W:].astype(jnp.float32)
            squares = real_amp * real_amp + imag_amp * imag_amp
            curvature = jnp.dot(squares, block[2] * power / (intensity * intensity), precision=highest)
            return (running[0] + projected, running[1] + curvature), intensity

        start = (jnp.zeros((2 * W, 2), jnp.float32), jnp.zeros((W,), jnp.float32))
        return lax.scan(data_step, start, data_blocks)

    coupling = couplings
    for iteration in range(ITERS):
        (projected, curvature), unused = data_pass(coupling)
        mixed_real = jnp.dot(gram_real, coupling[0], precision=highest) - jnp.dot(gram_imag, coupling[1], precision=highest)
        mixed_imag = jnp.dot(gram_real, coupling[1], precision=highest) + jnp.dot(gram_imag, coupling[0], precision=highest)
        grad_real = -(projected[:W, 0] + projected[W:, 1]) * inverse_count + mixed_real
        grad_imag = -(projected[:W, 1] - projected[W:, 0]) * inverse_count + mixed_imag
        total_curve = curvature * inverse_count + row_weight
        coupling = coupling - jnp.stack([grad_real, grad_imag]) / total_curve[None, :]
    unused, intensity = data_pass(coupling)
    return coupling, intensity.reshape(EVENTS_DATA)
```

```python
import jax
import jax.numpy as jnp
from jax import lax
from jax.sharding import Mesh, PartitionSpec as P

ITERS = 3
BACKGROUND = 0.5
ZX = ("z", "x")
EVENT = ("z", "x", "core")
PEERS = ("core", "wrow")


def share(values, axes, count):
    spread = jnp.broadcast_to(values[None], (count,) + values.shape)
    return lax.all_to_all(spread, axes, 0, 0)


def split3(values):
    high = lax.reduce_precision(values, 8, 7)
    rest = values - high
    middle = lax.reduce_precision(rest, 8, 7)
    low = rest - middle
    return [part.astype(jnp.bfloat16) for part in (high, middle, low)]


def pair_parameters(res_mass, res_width, local_wave, wave_count):
    owner = local_wave[None, :] == jnp.arange(wave_count, dtype=jnp.int32)[:, None]
    index = jnp.arange(res_mass.shape[0], dtype=jnp.int32)[None, :]
    first_at = jnp.min(jnp.where(owner, index, res_mass.shape[0]), axis=1, keepdims=True)
    first = owner & (index == first_at)
    second = owner & (index != first_at)
    square = (res_mass * res_mass)[None, :]
    product = (res_mass * res_width)[None, :]
    zero = jnp.float32(0.0)
    return [
        jnp.sum(jnp.where(mask, value, zero), axis=1)
        for mask in (first, second)
        for value in (square, product)
    ]


def amplitudes(mass_sq, angular_basis, table):
    square_a, product_a, square_b, product_b, angular_index = (row[:, None] for row in table)
    levels = jnp.arange(angular_basis.shape[0], dtype=jnp.float32)[None, :]
    chooser = (angular_index == levels).astype(jnp.bfloat16)
    angular = jnp.dot(chooser, angular_basis, preferred_element_type=jnp.float32)
    gap_a = square_a - mass_sq[None, :]
    gap_b = square_b - mass_sq[None, :]
    power_a = product_a * product_a
    power_b = product_b * product_b
    den_a = gap_a * gap_a + power_a
    den_b = gap_b * gap_b + power_b
    scale = angular / (den_a * den_b)
    real = (product_a * gap_a * den_b + product_b * gap_b * den_a) * scale
    imag = (power_a * den_b + power_b * den_a) * scale
    return jnp.stack([real, imag]).astype(jnp.bfloat16)


def shards(
    mc_mass, mc_basis, data_mass, data_basis, data_weight, res_mass, res_width, res_wave, wave_q, couplings
):
    own = wave_q.shape[0]
    rows = lax.axis_size("wrow")
    waves = own * rows
    zx = lax.axis_size("z") * lax.axis_size("x")
    events = zx * lax.axis_size("core")
    row = lax.axis_index("wrow")
    place = lax.axis_index(EVENT)
    own_table = pair_parameters(res_mass, res_width, res_wave - row * own, own)
    own_table = own_table + [wave_q.astype(jnp.float32), couplings[0], couplings[1], jnp.zeros((own,), jnp.float32)]
    gathered = share(jnp.stack(own_table).reshape(-1, 128), ("wrow",), rows)
    table = gathered.reshape(rows, 8, own).transpose(1, 0, 2).reshape(8, waves)
    mc_amp = amplitudes(mc_mass, mc_basis, table[:5])
    mc_rows = lax.dynamic_slice_in_dim(mc_amp, row * own, own, 1).reshape(2 * own, -1)
    products = lax.dot_general(
        mc_rows, mc_amp.reshape(2 * waves, -1), (((1,), (1,)), ((), ())), preferred_element_type=jnp.float32
    )
    normalize = 1.0 / (mc_mass.shape[0] * events)
    tile_real = products[:own, :waves] + products[own:, waves:]
    tile_imag = products[:own, waves:] - products[own:, :waves]
    tile = jnp.concatenate([tile_real, tile_imag], axis=1) * normalize
    pieces = lax.all_to_all(tile.astype(jnp.bfloat16).reshape(own, 8, -1), EVENT, 0, 0)
    gram_row = jnp.sum(pieces.astype(jnp.float32), axis=0).reshape(2, waves)
    data_amp = amplitudes(data_mass, data_basis, table[:5])
    stacked = data_amp.reshape(2 * waves, -1)
    block = lax.dynamic_slice_in_dim(data_amp, row * own, own, 1).astype(jnp.float32)
    squares = block[0] * block[0] + block[1] * block[1]
    inverse_count = 1.0 / (data_mass.shape[0] * events)
    mine = (jnp.arange(own, dtype=jnp.int32) == place).astype(jnp.float32)

    def field_of(coupling):
        kernel = jnp.stack(
            [
                jnp.concatenate([coupling[0], -coupling[1]]),
                jnp.concatenate([coupling[1], coupling[0]]),
            ]
        )
        parts = jnp.dot(jnp.concatenate(split3(kernel)), stacked, preferred_element_type=jnp.float32)
        return (parts[4:6] + parts[2:4]) + parts[0:2]

    coupling = table[5:7]
    row_weight = None
    for iteration in range(ITERS):
        field = field_of(coupling)
        power = field[0] * field[0] + field[1] * field[1]
        intensity = power + BACKGROUND
        weighting = data_weight / intensity
        carried = field * weighting
        curving = weighting * power / intensity
        grad_real = -jnp.sum(block[0] * carried[0] + block[1] * carried[1], axis=1) * inverse_count
        grad_imag = -jnp.sum(block[0] * carried[1] - block[1] * carried[0], axis=1) * inverse_count
        curve = jnp.sum(squares * curving, axis=1) * inverse_count
        mixed_real = jnp.sum(gram_row[0] * coupling[0] - gram_row[1] * coupling[1])
        mixed_imag = jnp.sum(gram_row[0] * coupling[1] + gram_row[1] * coupling[0])
        terms = [grad_real + mine * mixed_real, grad_imag + mine * mixed_imag, curve]
        terms.append(mine * jnp.sum(jnp.abs(gram_row)) if row_weight is None else jnp.zeros_like(curve))
        nearby = jnp.sum(share(jnp.stack(terms).reshape(-1, 128), ZX, zx), axis=0)
        everyone = share(nearby, PEERS, 2 * rows)
        total = jnp.sum(everyone.reshape(2, rows, 4, own), axis=0).transpose(1, 0, 2).reshape(4, waves)
        if row_weight is None:
            row_weight = total[3]
        coupling = coupling - total[:2] / (total[2] + row_weight)[None, :]
    field = field_of(coupling)
    intensity = field[0] * field[0] + field[1] * field[1] + BACKGROUND
    return (lax.dynamic_slice_in_dim(coupling, row * own, own, 1), intensity)


def solution(mesh):
    chips = Mesh(mesh.devices.reshape(4, 8, 2, 8), ("z", "x", "core", "wrow"))
    placed = (
        P(EVENT),
        P(None, EVENT),
        P(EVENT),
        P(None, EVENT),
        P(EVENT),
        P("wrow"),
        P("wrow"),
        P("wrow"),
        P("wrow"),
        P(None, "wrow"),
    )
    return jax.shard_map(
        shards, mesh=chips, in_specs=placed, out_specs=(P(None, "wrow"), P(EVENT)), check_vma=False
    )
```

```python
import functools

import jax
import jax.numpy as jnp
from jax import lax
from jax.experimental import pallas as pl
from jax.experimental.pallas import tpu as pltpu
from jax.sharding import Mesh, PartitionSpec as P

ITERS = 3
BACKGROUND = 0.5
ZX = ("z", "x")
EVENT = ("z", "x", "core")
PEERS = ("core", "wrow")
OWN = 64
LANES = 128
TILE = 256
CHUNK = 16
PARAMS = 6
VMEM_LIMIT = 24 << 20


def prepare_kernel(mass_ref, width_ref, wave_ref, level_ref, coupling_ref, place_ref, out_ref):
    count = mass_ref.shape[1]
    local = wave_ref[...] - place_ref[0] * OWN
    index = lax.broadcasted_iota(jnp.int32, (OWN, count), 1)
    owner = lax.broadcasted_iota(jnp.int32, (OWN, count), 0) == local
    first_at = jnp.min(jnp.where(owner, index, count), axis=1, keepdims=True)
    first = owner & (index == first_at)
    second = owner & (index != first_at)
    mass = mass_ref[...]
    square = mass * mass
    product = mass * width_ref[...]
    columns = [
        jnp.sum(jnp.where(mask, value, 0.0), axis=1, keepdims=True)
        for mask in (first, second)
        for value in (square, product)
    ]
    lane = lax.broadcasted_iota(jnp.int32, (OWN, LANES), 1)
    table = jnp.zeros((OWN, LANES), jnp.float32)
    for place, column in enumerate(columns):
        table = jnp.where(lane == place, column, table)
    turned = jnp.concatenate([table, jnp.zeros((LANES - OWN, LANES), jnp.float32)], axis=0).T
    rest = jnp.concatenate(
        [level_ref[...].astype(jnp.float32), coupling_ref[...], jnp.zeros((1, OWN), jnp.float32)], axis=0
    )
    rows = jnp.concatenate([turned[0:4, 0:OWN], rest], axis=1)
    send_terms(rows, out_ref)


def load_table(table_ref, wide_ref, chooser_ref):
    blocks = table_ref.shape[0]
    levels = chooser_ref.shape[1]
    for block in range(blocks):
        turned = jnp.concatenate([table_ref[block], jnp.zeros((LANES - 4, LANES), jnp.float32)], axis=0).T
        square_a, product_a, square_b, product_b = (turned[0:OWN, k : k + 1] for k in range(4))
        level = turned[OWN : 2 * OWN, 0:1]
        values = (
            square_a,
            square_b,
            product_a * square_b + product_b * square_a,
            product_a + product_b,
            product_a * product_b,
            2.0 * product_a * product_b,
        )
        rows = slice(block * OWN, (block + 1) * OWN)
        for place, value in enumerate(values):
            wide_ref[place, rows, :] = jnp.broadcast_to(value, (OWN, LANES))
        column = lax.broadcasted_iota(jnp.int32, (OWN, levels), 1).astype(jnp.float32)
        chooser_ref[rows, :] = (level == column).astype(jnp.bfloat16)


def fill_tile(mass_row, basis_tile, wide_ref, chooser_ref, store):
    waves = chooser_ref.shape[0]
    for start in range(0, waves, OWN):
        angular = jnp.dot(chooser_ref[start : start + OWN, :], basis_tile, preferred_element_type=jnp.float32)
        for inner in range(0, OWN, CHUNK):
            rows = slice(start + inner, start + inner + CHUNK)
            for half in range(0, TILE, LANES):
                mass = mass_row[:, half : half + LANES]
                gap = wide_ref[0, rows, :] - mass
                other = wide_ref[1, rows, :] - mass
                mixed = wide_ref[2, rows, :] - wide_ref[3, rows, :] * mass
                cross = gap * other
                pair = wide_ref[4, rows, :]
                lower = cross - pair
                mixed_square = mixed * mixed
                scale = angular[inner : inner + CHUNK, half : half + LANES] / (mixed_square + lower * lower)
                real = mixed * (cross + pair) * scale
                imag = (mixed_square - wide_ref[5, rows, :] * lower) * scale
                store(2 * start + inner, half, real.astype(jnp.bfloat16), imag.astype(jnp.bfloat16))


def gram_kernel(scale, table_ref, mass_ref, basis_ref, place_ref, out_ref, wide_ref, chooser_ref, amp_ref, sum_ref, turn_ref):
    load_table(table_ref, wide_ref, chooser_ref)
    sum_ref[...] = jnp.zeros_like(sum_ref)
    blocks = table_ref.shape[0]

    def store(row, half, real, imag):
        amp_ref[row : row + CHUNK, half : half + LANES] = real
        amp_ref[row + OWN : row + OWN + CHUNK, half : half + LANES] = imag

    @pl.loop(0, mass_ref.shape[1] // TILE)
    def _(step):
        columns = pl.ds(pl.multiple_of(step * TILE, TILE), TILE)
        fill_tile(mass_ref[:, columns], basis_ref[:, columns], wide_ref, chooser_ref, store)
        own = amp_ref[pl.ds(pl.multiple_of(place_ref[0] * 2 * OWN, 2 * OWN), 2 * OWN), :]
        sum_ref[...] += lax.dot_general(
            amp_ref[...], own, (((1,), (1,)), ((), ())), preferred_element_type=jnp.float32
        )

    for block in range(blocks):
        real_rows = sum_ref[2 * block * OWN : (2 * block + 1) * OWN, :]
        imag_rows = sum_ref[(2 * block + 1) * OWN : (2 * block + 2) * OWN, :]
        gram_real = real_rows + pltpu.roll(imag_rows, OWN, 1)
        gram_imag = imag_rows - pltpu.roll(real_rows, OWN, 1)
        turned = (jnp.concatenate([gram_real, gram_imag], axis=0) * scale).T
        turn_ref[:, block, :] = turned[0:OWN, :]
    out_ref[...] = turn_ref[...].astype(jnp.bfloat16)


def load_coupling(coupling, parts_ref):
    blocks = coupling.shape[0]
    signed, swapped = signs(coupling)
    parts_ref[...] = jnp.zeros_like(parts_ref)
    for row, value in enumerate((signed, swapped)):
        high = value.astype(jnp.bfloat16)
        rest = value - high.astype(jnp.float32)
        middle = rest.astype(jnp.bfloat16)
        low = (rest - middle.astype(jnp.float32)).astype(jnp.bfloat16)
        for place, part in enumerate((high, middle, low)):
            wide = part.astype(jnp.float32)
            for block in range(blocks):
                parts_ref[2 * place + row : 2 * place + row + 1, block * LANES : (block + 1) * LANES] = wide[block : block + 1]
    return signed, swapped


def field_of(parts, amp_tile):
    sums = jnp.dot(parts, amp_tile, preferred_element_type=jnp.float32)
    real = (sums[4:5] + sums[2:3]) + sums[0:1]
    imag = (sums[5:6] + sums[3:4]) + sums[1:2]
    return real, imag


def project_tile(real, imag, weight, own_tile, by_real_ref, by_imag_ref, curve_ref):
    power = real * real + imag * imag
    inverse = 1.0 / (power + BACKGROUND)
    weighting = weight * inverse
    real = real * weighting
    imag = imag * weighting
    curving = weighting * power * inverse
    for start in range(0, own_tile.shape[0], CHUNK):
        rows = slice(start, start + CHUNK)
        by_real = by_real_ref[rows, :]
        by_imag = by_imag_ref[rows, :]
        curve = curve_ref[rows, :]
        for half in range(0, own_tile.shape[1], LANES):
            lanes = slice(half, half + LANES)
            value = own_tile[rows, lanes].astype(jnp.float32)
            by_real = by_real + value * real[:, lanes]
            by_imag = by_imag + value * imag[:, lanes]
            curve = curve + value * value * curving[:, lanes]
        by_real_ref[rows, :] = by_real
        by_imag_ref[rows, :] = by_imag
        curve_ref[rows, :] = curve


def gradient_rows(scale, by_real_ref, by_imag_ref, curve_ref):
    low, high = slice(0, OWN), slice(OWN, 2 * OWN)
    grad = jnp.concatenate(
        [-(by_real_ref[low, :] + by_imag_ref[high, :]), by_real_ref[high, :] - by_imag_ref[low, :]], axis=0
    )
    curve = jnp.concatenate([curve_ref[low, :] + curve_ref[high, :], jnp.zeros((OWN, LANES), jnp.float32)], axis=0)
    grad_row = jnp.sum(grad.T, axis=0, keepdims=True) * scale
    curve_row = jnp.sum(curve.T, axis=0, keepdims=True) * scale
    return jnp.concatenate([grad_row, curve_row], axis=0)


def gram_rows(gram, signed, swapped, place_ref):
    mixed_real = jnp.sum(gram * signed, keepdims=True)
    mixed_imag = jnp.sum(gram * swapped, keepdims=True)
    row_weight = jnp.sum(jnp.abs(gram), keepdims=True)
    lane = lax.broadcasted_iota(jnp.int32, (1, LANES), 1)
    here = place_ref[1]
    grad_row = jnp.where(lane == here, mixed_real, 0.0) + jnp.where(lane == here + OWN, mixed_imag, 0.0)
    curve_row = jnp.where(lane == here + OWN, row_weight, 0.0)
    return jnp.concatenate([grad_row, curve_row], axis=0)


def signs(coupling):
    lane = lax.broadcasted_iota(jnp.int32, coupling.shape, 1)
    return jnp.where(lane < OWN, coupling, -coupling), pltpu.roll(coupling, OWN, 1)


def send_terms(terms, out_ref):
    for peer in range(out_ref.shape[0]):
        out_ref[peer] = terms


def merge_kernel(received_ref, out_ref):
    send_terms(jnp.sum(received_ref[...], axis=0), out_ref)


def clear(*refs):
    for ref in refs:
        ref[...] = jnp.zeros_like(ref)


def own_rows(place_ref):
    return pl.ds(pl.multiple_of(place_ref[0] * 2 * OWN, 2 * OWN), 2 * OWN)


def first_kernel(
    scale, table_ref, mass_ref, basis_ref, weight_ref, place_ref, pieces_ref, out_ref, coupling_ref, amp_ref, gram_ref,
    wide_ref, chooser_ref, parts_ref, by_real_ref, by_imag_ref, curve_ref
):
    load_table(table_ref, wide_ref, chooser_ref)
    for block in range(table_ref.shape[0]):
        half = table_ref[block]
        coupling_ref[block : block + 1, :] = jnp.concatenate([half[1:2, OWN:LANES], half[2:3, OWN:LANES]], axis=1)
    signed, swapped = load_coupling(coupling_ref[...], parts_ref)
    parts = parts_ref[...].astype(jnp.bfloat16)
    clear(by_real_ref, by_imag_ref, curve_ref)

    @pl.loop(0, mass_ref.shape[1] // TILE)
    def _(step):
        origin = pl.multiple_of(step * TILE, TILE)
        columns = pl.ds(origin, TILE)

        def store(row, half, real, imag):
            lanes = pl.ds(pl.multiple_of(origin + half, LANES), LANES)
            amp_ref[row : row + CHUNK, lanes] = real
            amp_ref[row + OWN : row + OWN + CHUNK, lanes] = imag

        fill_tile(mass_ref[:, columns], basis_ref[:, columns], wide_ref, chooser_ref, store)
        real, imag = field_of(parts, amp_ref[:, columns])
        own = amp_ref[own_rows(place_ref), columns]
        project_tile(real, imag, weight_ref[:, columns], own, by_real_ref, by_imag_ref, curve_ref)

    gram = jnp.sum(pieces_ref[...].astype(jnp.float32), axis=0)
    gram_ref[...] = gram
    terms = gradient_rows(scale, by_real_ref, by_imag_ref, curve_ref)
    send_terms(terms + gram_rows(gram, signed, swapped, place_ref), out_ref)


def new_coupling(received_ref, coupling_ref):
    blocks = coupling_ref.shape[0]
    total = received_ref[0:blocks] + received_ref[blocks : 2 * blocks]
    grad = total[:, 0, :]
    curve = total[:, 1, :]
    return coupling_ref[...] - grad / (curve + pltpu.roll(curve, OWN, 1))


def next_kernel(
    scale, received_ref, old_ref, amp_ref, weight_ref, place_ref, gram_ref, out_ref, coupling_ref,
    parts_ref, by_real_ref, by_imag_ref, curve_ref
):
    coupling = new_coupling(received_ref, old_ref)
    coupling_ref[...] = coupling
    signed, swapped = load_coupling(coupling, parts_ref)
    parts = parts_ref[...].astype(jnp.bfloat16)
    clear(by_real_ref, by_imag_ref, curve_ref)

    @pl.loop(0, amp_ref.shape[1] // (2 * TILE))
    def _(step):
        columns = pl.ds(pl.multiple_of(step * 2 * TILE, 2 * TILE), 2 * TILE)
        real, imag = field_of(parts, amp_ref[:, columns])
        own = amp_ref[own_rows(place_ref), columns]
        project_tile(real, imag, weight_ref[:, columns], own, by_real_ref, by_imag_ref, curve_ref)

    terms = gradient_rows(scale, by_real_ref, by_imag_ref, curve_ref)
    send_terms(terms + gram_rows(gram_ref[...], signed, swapped, place_ref), out_ref)


def last_kernel(received_ref, old_ref, amp_ref, place_ref, coupling_out_ref, intensity_ref, parts_ref, coupling_ref):
    coupling = new_coupling(received_ref, old_ref)
    coupling_ref[...] = coupling
    load_coupling(coupling, parts_ref)
    parts = parts_ref[...].astype(jnp.bfloat16)
    mine = coupling_ref[pl.ds(place_ref[0], 1), :]
    coupling_out_ref[0:1, :] = mine[:, 0:OWN]
    coupling_out_ref[1:2, :] = pltpu.roll(mine, OWN, 1)[:, 0:OWN]

    @pl.loop(0, amp_ref.shape[1] // (2 * TILE))
    def _(step):
        columns = pl.ds(pl.multiple_of(step * 2 * TILE, 2 * TILE), 2 * TILE)
        real, imag = field_of(parts, amp_ref[:, columns])
        intensity_ref[:, columns] = real * real + imag * imag + BACKGROUND


def call(kernel, outs, scratch, *args, smem):
    specs = [pl.BlockSpec(memory_space=pltpu.SMEM if place in smem else pltpu.VMEM) for place in range(len(args))]
    single = not isinstance(outs, tuple)
    return pl.pallas_call(
        kernel,
        out_shape=outs,
        in_specs=specs,
        out_specs=pl.BlockSpec(memory_space=pltpu.VMEM) if single else tuple(pl.BlockSpec(memory_space=pltpu.VMEM) for _ in outs),
        scratch_shapes=scratch,
        compiler_params=pltpu.CompilerParams(vmem_limit_bytes=VMEM_LIMIT),
    )(*args)


def shape(*dims, dtype=jnp.float32):
    return jax.ShapeDtypeStruct(dims, dtype)


def table_scratch(waves, levels):
    return [pltpu.VMEM((PARAMS, waves, LANES), jnp.float32), pltpu.VMEM((waves, levels), jnp.bfloat16)]


def pass_scratch(waves):
    return [pltpu.VMEM((8, 2 * waves), jnp.float32)] + [pltpu.VMEM((2 * OWN, LANES), jnp.float32) for _ in range(3)]


def shards(
    mc_mass, mc_basis, data_mass, data_basis, data_weight, res_mass, res_width, res_wave, wave_q, couplings
):
    rows = lax.axis_size("wrow")
    waves = OWN * rows
    zx = lax.axis_size("z") * lax.axis_size("x")
    events = zx * lax.axis_size("core")
    levels = mc_basis.shape[0]
    mc_count, data_count = mc_mass.shape[0], data_mass.shape[0]
    places = jnp.stack([lax.axis_index("wrow"), lax.axis_index(EVENT)]).astype(jnp.int32)
    own_table = call(
        prepare_kernel,
        shape(rows, 4, LANES),
        [],
        res_mass[None], res_width[None], res_wave[None], wave_q[None], couplings, places,
        smem=(5,),
    )
    table = lax.all_to_all(own_table, "wrow", 0, 0)
    tile = call(
        functools.partial(gram_kernel, 1.0 / (mc_count * events)),
        shape(OWN, rows, LANES, dtype=jnp.bfloat16),
        table_scratch(waves, levels)
        + [
            pltpu.VMEM((2 * waves, TILE), jnp.bfloat16),
            pltpu.VMEM((2 * waves, LANES), jnp.float32),
            pltpu.VMEM((OWN, rows, LANES), jnp.float32),
        ],
        table, mc_mass[None], mc_basis, places,
        smem=(3,),
    )
    pieces = lax.all_to_all(tile, EVENT, 0, 0)
    weight = data_weight[None]
    inverse_count = 1.0 / (data_count * events)
    amp_shape = pltpu.VMEM((2 * waves, data_count), jnp.bfloat16)
    terms, coupling, amp, gram_row = call(
        functools.partial(first_kernel, inverse_count),
        (shape(zx, 2, LANES), shape(rows, LANES), amp_shape, shape(rows, LANES)),
        table_scratch(waves, levels) + pass_scratch(waves),
        table, data_mass[None], data_basis, weight, places, pieces,
        smem=(4,),
    )

    def exchange(values):
        merged = call(merge_kernel, shape(2 * rows, 2, LANES), [], lax.all_to_all(values, ZX, 0, 0), smem=())
        return lax.all_to_all(merged, PEERS, 0, 0)

    for _ in range(1, ITERS):
        received = exchange(terms)
        terms, coupling = call(
            functools.partial(next_kernel, inverse_count),
            (shape(zx, 2, LANES), shape(rows, LANES)),
            pass_scratch(waves),
            received, coupling, amp, weight, places, gram_row,
            smem=(4,),
        )
    received = exchange(terms)
    coupling_out, intensity = call(
        last_kernel,
        (shape(2, OWN), shape(1, data_count)),
        [pltpu.VMEM((8, 2 * waves), jnp.float32), pltpu.VMEM((rows, LANES), jnp.float32)],
        received, coupling, amp, places,
        smem=(3,),
    )
    return coupling_out, intensity.reshape(data_count)


def solution(mesh):
    chips = Mesh(mesh.devices.reshape(4, 8, 2, 8), ("z", "x", "core", "wrow"))
    placed = (
        P(EVENT),
        P(None, EVENT),
        P(EVENT),
        P(None, EVENT),
        P(EVENT),
        P("wrow"),
        P("wrow"),
        P("wrow"),
        P("wrow"),
        P(None, "wrow"),
    )
    return jax.shard_map(
        shards, mesh=chips, in_specs=placed, out_specs=(P(None, "wrow"), P(EVENT)), check_vma=False
    )
```

```python
import functools

import jax
import jax.numpy as jnp
from jax import lax
from jax.experimental import pallas as pl
from jax.experimental.pallas import tpu as pltpu
from jax.sharding import Mesh, PartitionSpec as P

ITERS = 3
BACKGROUND = 0.5
ZX = ("z", "x")
EVENT = ("z", "x", "core")
PEERS = ("core", "wrow")
OWN = 64
LANES = 128
TILE = 512
CHUNK = 16
ROWS = 8
PARAMS = 6
VMEM_LIMIT = 24 << 20


def prepare_kernel(
    mass_in, width_in, wave_in, level_in, coupling_in, mc_mass_in, mc_basis_in, data_mass_in, data_basis_in,
    weight_in, place_ref, out_ref, mc_mass_out, mc_basis_out, data_mass_out, data_basis_out, weight_out,
    mass_ref, width_ref, wave_ref, level_ref, coupling_ref, small_sems, large_sems
):
    small = [
        pltpu.make_async_copy(source, target, small_sems.at[place])
        for place, (source, target) in enumerate(
            (
                (mass_in, mass_ref),
                (width_in, width_ref),
                (wave_in, wave_ref),
                (level_in, level_ref),
                (coupling_in, coupling_ref),
            )
        )
    ]
    large = [
        pltpu.make_async_copy(source, target, large_sems.at[place])
        for place, (source, target) in enumerate(
            (
                (mc_mass_in, mc_mass_out),
                (mc_basis_in, mc_basis_out),
                (data_mass_in, data_mass_out),
                (data_basis_in, data_basis_out),
                (weight_in, weight_out),
            )
        )
    ]
    for copy in small + large:
        copy.start()
    for copy in small:
        copy.wait()
    count = mass_ref.shape[1]
    local = wave_ref[...] - place_ref[0] * OWN
    index = lax.broadcasted_iota(jnp.int32, (OWN, count), 1)
    owner = lax.broadcasted_iota(jnp.int32, (OWN, count), 0) == local
    first_at = jnp.min(jnp.where(owner, index, count), axis=1, keepdims=True)
    first = owner & (index == first_at)
    second = owner & (index != first_at)
    mass = mass_ref[...]
    square = mass * mass
    product = mass * width_ref[...]
    columns = [
        jnp.sum(jnp.where(mask, value, 0.0), axis=1, keepdims=True)
        for mask in (first, second)
        for value in (square, product)
    ]
    lane = lax.broadcasted_iota(jnp.int32, (OWN, LANES), 1)
    table = jnp.zeros((OWN, LANES), jnp.float32)
    for place, column in enumerate(columns):
        table = jnp.where(lane == place, column, table)
    turned = jnp.concatenate([table, jnp.zeros((LANES - OWN, LANES), jnp.float32)], axis=0).T
    rest = jnp.concatenate(
        [level_ref[...].astype(jnp.float32), coupling_ref[...], jnp.zeros((1, OWN), jnp.float32)], axis=0
    )
    rows = jnp.concatenate([turned[0:4, 0:OWN], rest], axis=1)
    send_terms(rows, out_ref)
    for copy in large:
        copy.wait()


def load_table(table_ref, wide_ref, chooser_ref):
    blocks = table_ref.shape[0]
    levels = chooser_ref.shape[1]
    stacked = [table_ref[block] for block in range(blocks)]
    stacked.append(jnp.zeros((LANES - 4 * blocks, LANES), jnp.float32))
    turned = jnp.concatenate(stacked, axis=0).T
    column = lax.broadcasted_iota(jnp.int32, (OWN, levels), 1).astype(jnp.float32)
    for block in range(blocks):
        rows = slice(block * OWN, (block + 1) * OWN)
        for pair in range(2):
            first = 4 * block + 2 * pair
            square = jnp.broadcast_to(turned[0:OWN, first : first + 1], (OWN, LANES))
            product = jnp.broadcast_to(turned[0:OWN, first + 1 : first + 2], (OWN, LANES))
            wide_ref[3 * pair, rows, :] = square
            wide_ref[3 * pair + 1, rows, :] = product * product
            wide_ref[3 * pair + 2, rows, :] = product
        level = turned[OWN : 2 * OWN, 4 * block : 4 * block + 1]
        chooser_ref[rows, :] = (level == column).astype(jnp.bfloat16)


def lineshapes(mass, wide_ref, rows):
    real = imag = None
    for pair in range(2):
        product = wide_ref[3 * pair + 2, rows, :]
        gap = wide_ref[3 * pair, rows, :] - mass
        quotient = product / (gap * gap + wide_ref[3 * pair + 1, rows, :])
        real = quotient * gap if real is None else real + quotient * gap
        imag = quotient * product if imag is None else imag + quotient * product
    return real, imag


def fill_tile(mass_row, basis_tile, wide_ref, chooser_ref, store):
    waves = chooser_ref.shape[0]
    masses = [
        jnp.broadcast_to(mass_row[:, half : half + LANES], (ROWS, LANES)) for half in range(0, TILE, LANES)
    ]
    for start in range(0, waves, OWN):
        angular = jnp.dot(chooser_ref[start : start + OWN, :], basis_tile, preferred_element_type=jnp.float32)
        for inner in range(0, OWN, ROWS):
            rows = slice(start + inner, start + inner + ROWS)
            reals, imags = [], []
            for half, mass in enumerate(masses):
                real, imag = lineshapes(mass, wide_ref, rows)
                scale = angular[inner : inner + ROWS, half * LANES : (half + 1) * LANES]
                reals.append(real * scale)
                imags.append(imag * scale)
            real = jnp.concatenate(reals, axis=1).astype(jnp.bfloat16)
            imag = jnp.concatenate(imags, axis=1).astype(jnp.bfloat16)
            store(2 * start + inner, real, imag)


def gram_kernel(scale, table_ref, mass_ref, basis_ref, place_ref, out_ref, wide_ref, chooser_ref, amp_ref, sum_ref, turn_ref):
    load_table(table_ref, wide_ref, chooser_ref)
    sum_ref[...] = jnp.zeros_like(sum_ref)
    blocks = table_ref.shape[0]

    def store(row, real, imag):
        amp_ref[row : row + ROWS, :] = real
        amp_ref[row + OWN : row + OWN + ROWS, :] = imag

    @pl.loop(0, mass_ref.shape[1] // TILE)
    def _(step):
        columns = pl.ds(pl.multiple_of(step * TILE, TILE), TILE)
        fill_tile(mass_ref[:, columns], basis_ref[:, columns], wide_ref, chooser_ref, store)
        own = amp_ref[pl.ds(pl.multiple_of(place_ref[0] * 2 * OWN, 2 * OWN), 2 * OWN), :]
        sum_ref[...] += lax.dot_general(
            amp_ref[...], own, (((1,), (1,)), ((), ())), preferred_element_type=jnp.float32
        )

    for block in range(blocks):
        real_rows = sum_ref[2 * block * OWN : (2 * block + 1) * OWN, :]
        imag_rows = sum_ref[(2 * block + 1) * OWN : (2 * block + 2) * OWN, :]
        gram_real = real_rows + pltpu.roll(imag_rows, OWN, 1)
        gram_imag = imag_rows - pltpu.roll(real_rows, OWN, 1)
        turned = (jnp.concatenate([gram_real, gram_imag], axis=0) * scale).T
        turn_ref[:, block, :] = turned[0:OWN, :]
    out_ref[...] = turn_ref[...].astype(jnp.bfloat16)


def load_coupling(coupling, parts_ref):
    blocks = coupling.shape[0]
    signed, swapped = signs(coupling)
    parts_ref[...] = jnp.zeros_like(parts_ref)
    for row, value in enumerate((signed, swapped)):
        high = value.astype(jnp.bfloat16)
        rest = value - high.astype(jnp.float32)
        middle = rest.astype(jnp.bfloat16)
        low = (rest - middle.astype(jnp.float32)).astype(jnp.bfloat16)
        for place, part in enumerate((high, middle, low)):
            wide = part.astype(jnp.float32)
            for block in range(blocks):
                parts_ref[2 * place + row : 2 * place + row + 1, block * LANES : (block + 1) * LANES] = wide[block : block + 1]
    return signed, swapped


def field_of(parts, amp_tile):
    sums = jnp.dot(parts, amp_tile, preferred_element_type=jnp.float32)
    real = (sums[4:5] + sums[2:3]) + sums[0:1]
    imag = (sums[5:6] + sums[3:4]) + sums[1:2]
    return real, imag


def project_tile(real, imag, weight, own_tile, by_real_ref, by_imag_ref, curve_ref):
    power = real * real + imag * imag
    inverse = 1.0 / (power + BACKGROUND)
    weighting = weight * inverse
    real = real * weighting
    imag = imag * weighting
    curving = weighting * power * inverse
    for start in range(0, own_tile.shape[0], CHUNK):
        rows = slice(start, start + CHUNK)
        by_real = by_real_ref[rows, :]
        by_imag = by_imag_ref[rows, :]
        curve = curve_ref[rows, :]
        for half in range(0, own_tile.shape[1], LANES):
            lanes = slice(half, half + LANES)
            value = own_tile[rows, lanes].astype(jnp.float32)
            by_real = by_real + value * real[:, lanes]
            by_imag = by_imag + value * imag[:, lanes]
            curve = curve + value * value * curving[:, lanes]
        by_real_ref[rows, :] = by_real
        by_imag_ref[rows, :] = by_imag
        curve_ref[rows, :] = curve


def gradient_rows(scale, by_real_ref, by_imag_ref, curve_ref):
    low, high = slice(0, OWN), slice(OWN, 2 * OWN)
    grad = jnp.concatenate(
        [-(by_real_ref[low, :] + by_imag_ref[high, :]), by_real_ref[high, :] - by_imag_ref[low, :]], axis=0
    )
    curve = jnp.concatenate([curve_ref[low, :] + curve_ref[high, :], jnp.zeros((OWN, LANES), jnp.float32)], axis=0)
    grad_row = jnp.sum(grad.T, axis=0, keepdims=True) * scale
    curve_row = jnp.sum(curve.T, axis=0, keepdims=True) * scale
    return jnp.concatenate([grad_row, curve_row], axis=0)


def gram_rows(gram, signed, swapped, place_ref):
    mixed_real = jnp.sum(gram * signed, keepdims=True)
    mixed_imag = jnp.sum(gram * swapped, keepdims=True)
    row_weight = jnp.sum(jnp.abs(gram), keepdims=True)
    lane = lax.broadcasted_iota(jnp.int32, (1, LANES), 1)
    here = place_ref[1]
    grad_row = jnp.where(lane == here, mixed_real, 0.0) + jnp.where(lane == here + OWN, mixed_imag, 0.0)
    curve_row = jnp.where(lane == here + OWN, row_weight, 0.0)
    return jnp.concatenate([grad_row, curve_row], axis=0)


def signs(coupling):
    lane = lax.broadcasted_iota(jnp.int32, coupling.shape, 1)
    return jnp.where(lane < OWN, coupling, -coupling), pltpu.roll(coupling, OWN, 1)


def send_terms(terms, out_ref):
    for peer in range(out_ref.shape[0]):
        out_ref[peer] = terms


def merge_kernel(received_ref, out_ref):
    send_terms(jnp.sum(received_ref[...], axis=0), out_ref)


def clear(*refs):
    for ref in refs:
        ref[...] = jnp.zeros_like(ref)


def own_rows(place_ref):
    return pl.ds(pl.multiple_of(place_ref[0] * 2 * OWN, 2 * OWN), 2 * OWN)


def first_kernel(
    scale, table_ref, wide_ref, chooser_ref, mass_ref, basis_ref, weight_ref, place_ref, pieces_ref,
    out_ref, coupling_ref, amp_ref, gram_ref, parts_ref, by_real_ref, by_imag_ref, curve_ref
):
    for block in range(table_ref.shape[0]):
        half = table_ref[block]
        coupling_ref[block : block + 1, :] = jnp.concatenate([half[1:2, OWN:LANES], half[2:3, OWN:LANES]], axis=1)
    signed, swapped = load_coupling(coupling_ref[...], parts_ref)
    parts = parts_ref[...].astype(jnp.bfloat16)
    clear(by_real_ref, by_imag_ref, curve_ref)

    @pl.loop(0, mass_ref.shape[1] // TILE)
    def _(step):
        columns = pl.ds(pl.multiple_of(step * TILE, TILE), TILE)

        def store(row, real, imag):
            amp_ref[row : row + ROWS, columns] = real
            amp_ref[row + OWN : row + OWN + ROWS, columns] = imag

        fill_tile(mass_ref[:, columns], basis_ref[:, columns], wide_ref, chooser_ref, store)
        real, imag = field_of(parts, amp_ref[:, columns])
        own = amp_ref[own_rows(place_ref), columns]
        project_tile(real, imag, weight_ref[:, columns], own, by_real_ref, by_imag_ref, curve_ref)

    gram = jnp.sum(pieces_ref[...].astype(jnp.float32), axis=0)
    gram_ref[...] = gram
    terms = gradient_rows(scale, by_real_ref, by_imag_ref, curve_ref)
    send_terms(terms + gram_rows(gram, signed, swapped, place_ref), out_ref)


def new_coupling(received_ref, coupling_ref):
    blocks = coupling_ref.shape[0]
    total = received_ref[0:blocks] + received_ref[blocks : 2 * blocks]
    grad = total[:, 0, :]
    curve = total[:, 1, :]
    return coupling_ref[...] - grad / (curve + pltpu.roll(curve, OWN, 1))


def next_kernel(
    scale, received_ref, old_ref, amp_ref, weight_ref, place_ref, gram_ref, out_ref, coupling_ref,
    parts_ref, by_real_ref, by_imag_ref, curve_ref
):
    coupling = new_coupling(received_ref, old_ref)
    coupling_ref[...] = coupling
    signed, swapped = load_coupling(coupling, parts_ref)
    parts = parts_ref[...].astype(jnp.bfloat16)
    clear(by_real_ref, by_imag_ref, curve_ref)

    @pl.loop(0, amp_ref.shape[1] // (TILE))
    def _(step):
        columns = pl.ds(pl.multiple_of(step * TILE, TILE), TILE)
        real, imag = field_of(parts, amp_ref[:, columns])
        own = amp_ref[own_rows(place_ref), columns]
        project_tile(real, imag, weight_ref[:, columns], own, by_real_ref, by_imag_ref, curve_ref)

    terms = gradient_rows(scale, by_real_ref, by_imag_ref, curve_ref)
    send_terms(terms + gram_rows(gram_ref[...], signed, swapped, place_ref), out_ref)


def last_kernel(received_ref, old_ref, amp_ref, place_ref, coupling_out_ref, intensity_ref, parts_ref, coupling_ref):
    coupling = new_coupling(received_ref, old_ref)
    coupling_ref[...] = coupling
    load_coupling(coupling, parts_ref)
    parts = parts_ref[...].astype(jnp.bfloat16)
    mine = coupling_ref[pl.ds(place_ref[0], 1), :]
    coupling_out_ref[0:1, :] = mine[:, 0:OWN]
    coupling_out_ref[1:2, :] = pltpu.roll(mine, OWN, 1)[:, 0:OWN]

    @pl.loop(0, amp_ref.shape[1] // (TILE))
    def _(step):
        columns = pl.ds(pl.multiple_of(step * TILE, TILE), TILE)
        real, imag = field_of(parts, amp_ref[:, columns])
        intensity_ref[:, columns] = real * real + imag * imag + BACKGROUND


def call(kernel, outs, scratch, *args, smem, hbm=()):
    def space(place):
        return pltpu.SMEM if place in smem else pltpu.HBM if place in hbm else pltpu.VMEM

    single = not isinstance(outs, tuple)
    whole = pl.BlockSpec(memory_space=pltpu.VMEM)
    return pl.pallas_call(
        kernel,
        out_shape=outs,
        in_specs=[pl.BlockSpec(memory_space=space(place)) for place in range(len(args))],
        out_specs=whole if single else tuple(whole for _ in outs),
        scratch_shapes=scratch,
        compiler_params=pltpu.CompilerParams(vmem_limit_bytes=VMEM_LIMIT),
    )(*(pltpu.with_memory_space_constraint(arg, pltpu.HBM) if place in hbm else arg for place, arg in enumerate(args)))


def shape(*dims, dtype=jnp.float32):
    return jax.ShapeDtypeStruct(dims, dtype)


def pass_scratch(waves):
    return [pltpu.VMEM((8, 2 * waves), jnp.float32)] + [pltpu.VMEM((2 * OWN, LANES), jnp.float32) for _ in range(3)]


def shards(
    mc_mass, mc_basis, data_mass, data_basis, data_weight, res_mass, res_width, res_wave, wave_q, couplings
):
    rows = lax.axis_size("wrow")
    waves = OWN * rows
    zx = lax.axis_size("z") * lax.axis_size("x")
    events = zx * lax.axis_size("core")
    levels = mc_basis.shape[0]
    mc_count, data_count = mc_mass.shape[0], data_mass.shape[0]
    places = jnp.stack([lax.axis_index("wrow"), lax.axis_index(EVENT)]).astype(jnp.int32)
    own_table, mc_mass, mc_basis, data_mass, data_basis, weight = call(
        prepare_kernel,
        (
            shape(rows, 4, LANES),
            shape(1, mc_count),
            shape(levels, mc_count, dtype=jnp.bfloat16),
            shape(1, data_count),
            shape(levels, data_count, dtype=jnp.bfloat16),
            shape(1, data_count),
        ),
        [
            pltpu.VMEM((1, res_mass.shape[0]), jnp.float32),
            pltpu.VMEM((1, res_width.shape[0]), jnp.float32),
            pltpu.VMEM((1, res_wave.shape[0]), jnp.int32),
            pltpu.VMEM((1, OWN), jnp.int32),
            pltpu.VMEM((2, OWN), jnp.float32),
            pltpu.SemaphoreType.DMA((5,)),
            pltpu.SemaphoreType.DMA((5,)),
        ],
        res_mass[None], res_width[None], res_wave[None], wave_q[None], couplings,
        mc_mass[None], mc_basis, data_mass[None], data_basis, data_weight[None], places,
        smem=(10,),
        hbm=range(10),
    )
    table = lax.all_to_all(own_table, "wrow", 0, 0)
    tile, wide, chooser = call(
        functools.partial(gram_kernel, 1.0 / (mc_count * events)),
        (
            shape(OWN, rows, LANES, dtype=jnp.bfloat16),
            shape(PARAMS, waves, LANES),
            shape(waves, levels, dtype=jnp.bfloat16),
        ),
        [
            pltpu.VMEM((2 * waves, TILE), jnp.bfloat16),
            pltpu.VMEM((2 * waves, LANES), jnp.float32),
            pltpu.VMEM((OWN, rows, LANES), jnp.float32),
        ],
        table, mc_mass, mc_basis, places,
        smem=(3,),
    )
    pieces = lax.all_to_all(tile, EVENT, 0, 0)
    inverse_count = 1.0 / (data_count * events)
    amp_shape = pltpu.VMEM((2 * waves, data_count), jnp.bfloat16)
    terms, coupling, amp, gram_row = call(
        functools.partial(first_kernel, inverse_count),
        (shape(zx, 2, LANES), shape(rows, LANES), amp_shape, shape(rows, LANES)),
        pass_scratch(waves),
        table, wide, chooser, data_mass, data_basis, weight, places, pieces,
        smem=(6,),
    )

    def exchange(values):
        merged = call(merge_kernel, shape(2 * rows, 2, LANES), [], lax.all_to_all(values, ZX, 0, 0), smem=())
        return lax.all_to_all(merged, PEERS, 0, 0)

    for _ in range(1, ITERS):
        received = exchange(terms)
        terms, coupling = call(
            functools.partial(next_kernel, inverse_count),
            (shape(zx, 2, LANES), shape(rows, LANES)),
            pass_scratch(waves),
            received, coupling, amp, weight, places, gram_row,
            smem=(4,),
        )
    received = exchange(terms)
    coupling_out, intensity = call(
        last_kernel,
        (shape(2, OWN), shape(1, data_count)),
        [pltpu.VMEM((8, 2 * waves), jnp.float32), pltpu.VMEM((rows, LANES), jnp.float32)],
        received, coupling, amp, places,
        smem=(3,),
    )
    return coupling_out, intensity.reshape(data_count)


def solution(mesh):
    chips = Mesh(mesh.devices.reshape(4, 8, 2, 8), ("z", "x", "core", "wrow"))
    placed = (
        P(EVENT),
        P(None, EVENT),
        P(EVENT),
        P(None, EVENT),
        P(EVENT),
        P("wrow"),
        P("wrow"),
        P("wrow"),
        P("wrow"),
        P(None, "wrow"),
    )
    return jax.shard_map(
        shards, mesh=chips, in_specs=placed, out_specs=(P(None, "wrow"), P(EVENT)), check_vma=False
    )
```

```python
import functools

import jax
import jax.numpy as jnp
from jax import lax
from jax.experimental import pallas as pl
from jax.experimental.pallas import tpu as pltpu
from jax.sharding import Mesh, PartitionSpec as P

ITERS = 3
BACKGROUND = 0.5
ZX = ("z", "x")
EVENT = ("z", "x", "core")
PEERS = ("core", "wrow")
OWN = 64
LANES = 128
TILE = 512
CHUNK = 16
ROWS = 8
PARAMS = 4
NEXT_ROWS = 256
LAST_ROWS = 256
VMEM_LIMIT = 24 << 20


def prepare_kernel(
    mass_in, width_in, wave_in, level_in, coupling_in, mc_mass_in, mc_basis_in, data_mass_in, data_basis_in,
    weight_in, place_ref, out_ref, mc_mass_out, mc_basis_out, data_mass_out, data_basis_out, weight_out,
    mass_ref, width_ref, wave_ref, level_ref, coupling_ref, small_sems, large_sems
):
    small = [
        pltpu.make_async_copy(source, target, small_sems.at[place])
        for place, (source, target) in enumerate(
            (
                (mass_in, mass_ref),
                (width_in, width_ref),
                (wave_in, wave_ref),
                (level_in, level_ref),
                (coupling_in, coupling_ref),
            )
        )
    ]
    large = [
        pltpu.make_async_copy(source, target, large_sems.at[place])
        for place, (source, target) in enumerate(
            (
                (mc_mass_in, mc_mass_out),
                (mc_basis_in, mc_basis_out),
                (data_mass_in, data_mass_out),
                (data_basis_in, data_basis_out),
                (weight_in, weight_out),
            )
        )
    ]
    for copy in small + large:
        copy.start()
    for copy in small:
        copy.wait()
    count = mass_ref.shape[1]
    local = wave_ref[...] - place_ref[0] * OWN
    index = lax.broadcasted_iota(jnp.int32, (OWN, count), 1)
    owner = lax.broadcasted_iota(jnp.int32, (OWN, count), 0) == local
    first_at = jnp.min(jnp.where(owner, index, count), axis=1, keepdims=True)
    first = owner & (index == first_at)
    second = owner & (index != first_at)
    mass = mass_ref[...]
    square = mass * mass
    inverse = 1.0 / (mass * width_ref[...])
    columns = [
        jnp.sum(jnp.where(mask, value, 0.0), axis=1, keepdims=True)
        for mask in (first, second)
        for value in (square, inverse)
    ]
    lane = lax.broadcasted_iota(jnp.int32, (OWN, LANES), 1)
    table = jnp.zeros((OWN, LANES), jnp.float32)
    for place, column in enumerate(columns):
        table = jnp.where(lane == place, column, table)
    turned = jnp.concatenate([table, jnp.zeros((LANES - OWN, LANES), jnp.float32)], axis=0).T
    rest = jnp.concatenate(
        [level_ref[...].astype(jnp.float32), coupling_ref[...], jnp.zeros((1, OWN), jnp.float32)], axis=0
    )
    rows = jnp.concatenate([turned[0:4, 0:OWN], rest], axis=1)
    send_terms(rows, out_ref)
    for copy in large:
        copy.wait()


def load_table(table_ref, wide_ref, chooser_ref):
    blocks = table_ref.shape[0]
    levels = chooser_ref.shape[1]
    stacked = [table_ref[block] for block in range(blocks)]
    stacked.append(jnp.zeros((LANES - 4 * blocks, LANES), jnp.float32))
    turned = jnp.concatenate(stacked, axis=0).T
    column = lax.broadcasted_iota(jnp.int32, (OWN, levels), 1).astype(jnp.float32)
    for block in range(blocks):
        rows = slice(block * OWN, (block + 1) * OWN)
        for pair in range(2):
            first = 4 * block + 2 * pair
            square = turned[0:OWN, first : first + 1]
            inverse = turned[0:OWN, first + 1 : first + 2]
            wide_ref[2 * pair, rows, :] = jnp.broadcast_to(square, (OWN, LANES))
            wide_ref[2 * pair + 1, rows, :] = jnp.broadcast_to(inverse, (OWN, LANES))
        level = turned[OWN : 2 * OWN, 4 * block : 4 * block + 1]
        chooser_ref[rows, :] = (level == column).astype(jnp.bfloat16)


def lineshapes(mass, wide_ref, rows):
    real = imag = None
    for pair in range(2):
        gap = (wide_ref[2 * pair, rows, :] - mass) * wide_ref[2 * pair + 1, rows, :]
        share = 1.0 / (gap * gap + 1.0)
        real = gap * share if real is None else real + gap * share
        imag = share if imag is None else imag + share
    return real, imag


def fill_tile(mass_row, basis_tile, wide_ref, chooser_ref, store):
    waves = chooser_ref.shape[0]
    masses = [
        jnp.broadcast_to(mass_row[:, half : half + LANES], (ROWS, LANES)) for half in range(0, TILE, LANES)
    ]
    for start in range(0, waves, OWN):
        angular = jnp.dot(chooser_ref[start : start + OWN, :], basis_tile, preferred_element_type=jnp.float32)
        for inner in range(0, OWN, ROWS):
            rows = slice(start + inner, start + inner + ROWS)
            reals, imags = [], []
            for half, mass in enumerate(masses):
                real, imag = lineshapes(mass, wide_ref, rows)
                scale = angular[inner : inner + ROWS, half * LANES : (half + 1) * LANES]
                reals.append(real * scale)
                imags.append(imag * scale)
            real = jnp.concatenate(reals, axis=1).astype(jnp.bfloat16)
            imag = jnp.concatenate(imags, axis=1).astype(jnp.bfloat16)
            store(2 * start + inner, real, imag)


def gram_kernel(scale, table_ref, mass_ref, basis_ref, place_ref, out_ref, wide_ref, chooser_ref, amp_ref, sum_ref, turn_ref):
    load_table(table_ref, wide_ref, chooser_ref)
    sum_ref[...] = jnp.zeros_like(sum_ref)
    blocks = table_ref.shape[0]

    def store(row, real, imag):
        amp_ref[row : row + ROWS, :] = real
        amp_ref[row + OWN : row + OWN + ROWS, :] = imag

    @pl.loop(0, mass_ref.shape[1] // TILE)
    def _(step):
        columns = pl.ds(pl.multiple_of(step * TILE, TILE), TILE)
        fill_tile(mass_ref[:, columns], basis_ref[:, columns], wide_ref, chooser_ref, store)
        own = amp_ref[pl.ds(pl.multiple_of(place_ref[0] * 2 * OWN, 2 * OWN), 2 * OWN), :]
        sum_ref[...] += lax.dot_general(
            amp_ref[...], own, (((1,), (1,)), ((), ())), preferred_element_type=jnp.float32
        )

    for block in range(blocks):
        real_rows = sum_ref[2 * block * OWN : (2 * block + 1) * OWN, :]
        imag_rows = sum_ref[(2 * block + 1) * OWN : (2 * block + 2) * OWN, :]
        gram_real = real_rows + pltpu.roll(imag_rows, OWN, 1)
        gram_imag = imag_rows - pltpu.roll(real_rows, OWN, 1)
        turned = (jnp.concatenate([gram_real, gram_imag], axis=0) * scale).T
        turn_ref[:, block, :] = turned[0:OWN, :]
    out_ref[...] = turn_ref[...].astype(jnp.bfloat16)


def load_coupling(coupling, parts_ref):
    blocks = coupling.shape[0]
    signed, swapped = signs(coupling)
    parts_ref[...] = jnp.zeros_like(parts_ref)
    for row, value in enumerate((signed, swapped)):
        high = value.astype(jnp.bfloat16)
        rest = value - high.astype(jnp.float32)
        middle = rest.astype(jnp.bfloat16)
        low = (rest - middle.astype(jnp.float32)).astype(jnp.bfloat16)
        for place, part in enumerate((high, middle, low)):
            wide = part.astype(jnp.float32)
            for block in range(blocks):
                parts_ref[2 * place + row : 2 * place + row + 1, block * LANES : (block + 1) * LANES] = wide[block : block + 1]
    return signed, swapped


def load_columns(signed, swapped, vector_rows, column_ref):
    blocks = vector_rows // LANES
    first = signed.shape[0] - blocks
    rows = [signed[first:], swapped[first:], jnp.zeros((LANES - 2 * blocks, LANES), jnp.float32)]
    turned = jnp.concatenate(rows, axis=0).T
    for place in range(2):
        for block in range(blocks):
            column = turned[:, place * blocks + block : place * blocks + block + 1]
            column_ref[place, block * LANES : (block + 1) * LANES, :] = jnp.broadcast_to(column, (LANES, LANES))


def field_of(parts, amp_ref, columns, column_ref=None):
    waves = amp_ref.shape[0]
    vector_rows = 0 if column_ref is None else column_ref.shape[1]
    matrix_rows = waves - vector_rows
    sums = jnp.dot(parts[:, :matrix_rows], amp_ref[:matrix_rows, columns], preferred_element_type=jnp.float32)
    real = (sums[4:5] + sums[2:3]) + sums[0:1]
    imag = (sums[5:6] + sums[3:4]) + sums[1:2]
    if vector_rows:
        lanes = TILE // LANES
        reals = [jnp.zeros((ROWS, LANES), jnp.float32) for _ in range(lanes)]
        imags = [jnp.zeros((ROWS, LANES), jnp.float32) for _ in range(lanes)]
        for start in range(0, vector_rows, ROWS):
            rows = slice(start, start + ROWS)
            values = amp_ref[matrix_rows + start : matrix_rows + start + ROWS, columns].astype(jnp.float32)
            by_real, by_imag = column_ref[0, rows, :], column_ref[1, rows, :]
            for place in range(lanes):
                value = values[:, place * LANES : (place + 1) * LANES]
                reals[place] = reals[place] + value * by_real
                imags[place] = imags[place] + value * by_imag
        real = real + jnp.sum(jnp.concatenate(reals, axis=1), axis=0, keepdims=True)
        imag = imag + jnp.sum(jnp.concatenate(imags, axis=1), axis=0, keepdims=True)
    return real, imag


def tile_at(step):
    return pl.ds(pl.multiple_of(step * TILE, TILE), TILE)


def project_tile(real, imag, weight, own_tile, by_real_ref, by_imag_ref, curve_ref):
    power = real * real + imag * imag
    inverse = 1.0 / (power + BACKGROUND)
    weighting = weight * inverse
    real = real * weighting
    imag = imag * weighting
    curving = weighting * power * inverse
    for start in range(0, own_tile.shape[0], CHUNK):
        rows = slice(start, start + CHUNK)
        by_real = by_real_ref[rows, :]
        by_imag = by_imag_ref[rows, :]
        curve = curve_ref[rows, :]
        for half in range(0, own_tile.shape[1], LANES):
            lanes = slice(half, half + LANES)
            value = own_tile[rows, lanes].astype(jnp.float32)
            by_real = by_real + value * real[:, lanes]
            by_imag = by_imag + value * imag[:, lanes]
            curve = curve + value * value * curving[:, lanes]
        by_real_ref[rows, :] = by_real
        by_imag_ref[rows, :] = by_imag
        curve_ref[rows, :] = curve


def gradient_rows(scale, by_real_ref, by_imag_ref, curve_ref):
    low, high = slice(0, OWN), slice(OWN, 2 * OWN)
    grad = jnp.concatenate(
        [-(by_real_ref[low, :] + by_imag_ref[high, :]), by_real_ref[high, :] - by_imag_ref[low, :]], axis=0
    )
    curve = jnp.concatenate([curve_ref[low, :] + curve_ref[high, :], jnp.zeros((OWN, LANES), jnp.float32)], axis=0)
    grad_row = jnp.sum(grad.T, axis=0, keepdims=True) * scale
    curve_row = jnp.sum(curve.T, axis=0, keepdims=True) * scale
    return jnp.concatenate([grad_row, curve_row], axis=0)


def gram_rows(gram, signed, swapped, place_ref):
    mixed_real = jnp.sum(gram * signed, keepdims=True)
    mixed_imag = jnp.sum(gram * swapped, keepdims=True)
    row_weight = jnp.sum(jnp.abs(gram), keepdims=True)
    lane = lax.broadcasted_iota(jnp.int32, (1, LANES), 1)
    here = place_ref[1]
    grad_row = jnp.where(lane == here, mixed_real, 0.0) + jnp.where(lane == here + OWN, mixed_imag, 0.0)
    curve_row = jnp.where(lane == here + OWN, row_weight, 0.0)
    return jnp.concatenate([grad_row, curve_row], axis=0)


def signs(coupling):
    lane = lax.broadcasted_iota(jnp.int32, coupling.shape, 1)
    return jnp.where(lane < OWN, coupling, -coupling), pltpu.roll(coupling, OWN, 1)


def send_terms(terms, out_ref):
    for peer in range(out_ref.shape[0]):
        out_ref[peer] = terms


def merge_kernel(received_ref, out_ref):
    send_terms(jnp.sum(received_ref[...], axis=0), out_ref)


def clear(*refs):
    for ref in refs:
        ref[...] = jnp.zeros_like(ref)


def own_rows(place_ref):
    return pl.ds(pl.multiple_of(place_ref[0] * 2 * OWN, 2 * OWN), 2 * OWN)


def first_kernel(
    scale, table_ref, wide_ref, chooser_ref, mass_ref, basis_ref, weight_ref, place_ref, pieces_ref,
    out_ref, coupling_ref, amp_ref, gram_ref, parts_ref, by_real_ref, by_imag_ref, curve_ref
):
    for block in range(table_ref.shape[0]):
        half = table_ref[block]
        coupling_ref[block : block + 1, :] = jnp.concatenate([half[1:2, OWN:LANES], half[2:3, OWN:LANES]], axis=1)
    signed, swapped = load_coupling(coupling_ref[...], parts_ref)
    parts = parts_ref[...].astype(jnp.bfloat16)
    clear(by_real_ref, by_imag_ref, curve_ref)

    @pl.loop(0, mass_ref.shape[1] // TILE)
    def _(step):
        columns = pl.ds(pl.multiple_of(step * TILE, TILE), TILE)

        def store(row, real, imag):
            amp_ref[row : row + ROWS, columns] = real
            amp_ref[row + OWN : row + OWN + ROWS, columns] = imag

        fill_tile(mass_ref[:, columns], basis_ref[:, columns], wide_ref, chooser_ref, store)
        real, imag = field_of(parts, amp_ref, columns)
        own = amp_ref[own_rows(place_ref), columns]
        project_tile(real, imag, weight_ref[:, columns], own, by_real_ref, by_imag_ref, curve_ref)

    gram = jnp.sum(pieces_ref[...].astype(jnp.float32), axis=0)
    gram_ref[...] = gram
    terms = gradient_rows(scale, by_real_ref, by_imag_ref, curve_ref)
    send_terms(terms + gram_rows(gram, signed, swapped, place_ref), out_ref)


def new_coupling(received_ref, coupling_ref):
    blocks = coupling_ref.shape[0]
    total = received_ref[0:blocks] + received_ref[blocks : 2 * blocks]
    grad = total[:, 0, :]
    curve = total[:, 1, :]
    return coupling_ref[...] - grad / (curve + pltpu.roll(curve, OWN, 1))


def next_kernel(
    scale, received_ref, old_ref, amp_ref, weight_ref, place_ref, gram_ref, out_ref, coupling_ref,
    parts_ref, by_real_ref, by_imag_ref, curve_ref, column_ref
):
    coupling = new_coupling(received_ref, old_ref)
    coupling_ref[...] = coupling
    signed, swapped = load_coupling(coupling, parts_ref)
    load_columns(signed, swapped, column_ref.shape[1], column_ref)
    parts = parts_ref[...].astype(jnp.bfloat16)
    clear(by_real_ref, by_imag_ref, curve_ref)
    tiles = amp_ref.shape[1] // TILE

    def project(step, field):
        own = amp_ref[own_rows(place_ref), tile_at(step)]
        project_tile(*field, weight_ref[:, tile_at(step)], own, by_real_ref, by_imag_ref, curve_ref)

    def ahead(step, field):
        later = field_of(parts, amp_ref, tile_at(step + 1), column_ref)
        project(step, field)
        return later

    field = lax.fori_loop(0, tiles - 1, ahead, field_of(parts, amp_ref, tile_at(0), column_ref))
    project(tiles - 1, field)
    terms = gradient_rows(scale, by_real_ref, by_imag_ref, curve_ref)
    send_terms(terms + gram_rows(gram_ref[...], signed, swapped, place_ref), out_ref)


def last_kernel(
    received_ref, old_ref, amp_ref, place_ref, coupling_out_ref, intensity_ref, parts_ref, coupling_ref, column_ref
):
    coupling = new_coupling(received_ref, old_ref)
    coupling_ref[...] = coupling
    signed, swapped = load_coupling(coupling, parts_ref)
    load_columns(signed, swapped, column_ref.shape[1], column_ref)
    parts = parts_ref[...].astype(jnp.bfloat16)
    mine = coupling_ref[pl.ds(place_ref[0], 1), :]
    coupling_out_ref[0:1, :] = mine[:, 0:OWN]
    coupling_out_ref[1:2, :] = pltpu.roll(mine, OWN, 1)[:, 0:OWN]

    @pl.loop(0, amp_ref.shape[1] // TILE)
    def _(step):
        real, imag = field_of(parts, amp_ref, tile_at(step), column_ref)
        intensity_ref[:, tile_at(step)] = real * real + imag * imag + BACKGROUND


def call(kernel, outs, scratch, *args, smem, hbm=()):
    def space(place):
        return pltpu.SMEM if place in smem else pltpu.HBM if place in hbm else pltpu.VMEM

    single = not isinstance(outs, tuple)
    whole = pl.BlockSpec(memory_space=pltpu.VMEM)
    return pl.pallas_call(
        kernel,
        out_shape=outs,
        in_specs=[pl.BlockSpec(memory_space=space(place)) for place in range(len(args))],
        out_specs=whole if single else tuple(whole for _ in outs),
        scratch_shapes=scratch,
        compiler_params=pltpu.CompilerParams(vmem_limit_bytes=VMEM_LIMIT),
    )(*(pltpu.with_memory_space_constraint(arg, pltpu.HBM) if place in hbm else arg for place, arg in enumerate(args)))


def shape(*dims, dtype=jnp.float32):
    return jax.ShapeDtypeStruct(dims, dtype)


def pass_scratch(waves):
    return [pltpu.VMEM((8, 2 * waves), jnp.float32)] + [pltpu.VMEM((2 * OWN, LANES), jnp.float32) for _ in range(3)]


def shards(
    mc_mass, mc_basis, data_mass, data_basis, data_weight, res_mass, res_width, res_wave, wave_q, couplings
):
    rows = lax.axis_size("wrow")
    waves = OWN * rows
    zx = lax.axis_size("z") * lax.axis_size("x")
    events = zx * lax.axis_size("core")
    levels = mc_basis.shape[0]
    mc_count, data_count = mc_mass.shape[0], data_mass.shape[0]
    places = jnp.stack([lax.axis_index("wrow"), lax.axis_index(EVENT)]).astype(jnp.int32)
    own_table, mc_mass, mc_basis, data_mass, data_basis, weight = call(
        prepare_kernel,
        (
            shape(rows, 4, LANES),
            shape(1, mc_count),
            shape(levels, mc_count, dtype=jnp.bfloat16),
            shape(1, data_count),
            shape(levels, data_count, dtype=jnp.bfloat16),
            shape(1, data_count),
        ),
        [
            pltpu.VMEM((1, res_mass.shape[0]), jnp.float32),
            pltpu.VMEM((1, res_width.shape[0]), jnp.float32),
            pltpu.VMEM((1, res_wave.shape[0]), jnp.int32),
            pltpu.VMEM((1, OWN), jnp.int32),
            pltpu.VMEM((2, OWN), jnp.float32),
            pltpu.SemaphoreType.DMA((5,)),
            pltpu.SemaphoreType.DMA((5,)),
        ],
        res_mass[None], res_width[None], res_wave[None], wave_q[None], couplings,
        mc_mass[None], mc_basis, data_mass[None], data_basis, data_weight[None], places,
        smem=(10,),
        hbm=range(10),
    )
    table = lax.all_to_all(own_table, "wrow", 0, 0)
    tile, wide, chooser = call(
        functools.partial(gram_kernel, 1.0 / (mc_count * events)),
        (
            shape(OWN, rows, LANES, dtype=jnp.bfloat16),
            shape(PARAMS, waves, LANES),
            shape(waves, levels, dtype=jnp.bfloat16),
        ),
        [
            pltpu.VMEM((2 * waves, TILE), jnp.bfloat16),
            pltpu.VMEM((2 * waves, LANES), jnp.float32),
            pltpu.VMEM((OWN, rows, LANES), jnp.float32),
        ],
        table, mc_mass, mc_basis, places,
        smem=(3,),
    )
    pieces = lax.all_to_all(tile, EVENT, 0, 0)
    inverse_count = 1.0 / (data_count * events)
    amp_shape = pltpu.VMEM((2 * waves, data_count), jnp.bfloat16)
    terms, coupling, amp, gram_row = call(
        functools.partial(first_kernel, inverse_count),
        (shape(zx, 2, LANES), shape(rows, LANES), amp_shape, shape(rows, LANES)),
        pass_scratch(waves),
        table, wide, chooser, data_mass, data_basis, weight, places, pieces,
        smem=(6,),
    )

    def exchange(values):
        merged = call(merge_kernel, shape(2 * rows, 2, LANES), [], lax.all_to_all(values, ZX, 0, 0), smem=())
        return lax.all_to_all(merged, PEERS, 0, 0)

    for _ in range(1, ITERS):
        received = exchange(terms)
        terms, coupling = call(
            functools.partial(next_kernel, inverse_count),
            (shape(zx, 2, LANES), shape(rows, LANES)),
            pass_scratch(waves) + [pltpu.VMEM((2, NEXT_ROWS, LANES), jnp.float32)],
            received, coupling, amp, weight, places, gram_row,
            smem=(4,),
        )
    received = exchange(terms)
    coupling_out, intensity = call(
        last_kernel,
        (shape(2, OWN), shape(1, data_count)),
        [
            pltpu.VMEM((8, 2 * waves), jnp.float32),
            pltpu.VMEM((rows, LANES), jnp.float32),
            pltpu.VMEM((2, LAST_ROWS, LANES), jnp.float32),
        ],
        received, coupling, amp, places,
        smem=(3,),
    )
    return coupling_out, intensity.reshape(data_count)


def solution(mesh):
    chips = Mesh(mesh.devices.reshape(4, 8, 2, 8), ("z", "x", "core", "wrow"))
    placed = (
        P(EVENT),
        P(None, EVENT),
        P(EVENT),
        P(None, EVENT),
        P(EVENT),
        P("wrow"),
        P("wrow"),
        P("wrow"),
        P("wrow"),
        P(None, "wrow"),
    )
    return jax.shard_map(
        shards, mesh=chips, in_specs=placed, out_specs=(P(None, "wrow"), P(EVENT)), check_vma=False
    )
```

```python
import functools

import jax
import jax.numpy as jnp
from jax import lax
from jax.experimental import pallas as pl
from jax.experimental.pallas import tpu as pltpu
from jax.sharding import Mesh, PartitionSpec as P

ITERS = 3
BACKGROUND = 0.5
ZX = ("z", "x")
EVENT = ("z", "x", "core")
PEERS = ("core", "wrow")
OWN = 64
LANES = 128
TILE = 512
CHUNK = 16
ROWS = 8
PARAMS = 4
NEXT_ROWS = 256
LAST_ROWS = 256
VMEM_LIMIT = 24 << 20


def copies(pairs, sems):
    started = [pltpu.make_async_copy(source, target, sems.at[place]) for place, (source, target) in enumerate(pairs)]
    for copy in started:
        copy.start()
    return started


def prepare_kernel(
    mass_in, width_in, wave_in, level_in, coupling_in, place_ref, out_ref,
    mass_ref, width_ref, wave_ref, level_ref, coupling_ref, sems
):
    pairs = (
        (mass_in, mass_ref),
        (width_in, width_ref),
        (wave_in, wave_ref),
        (level_in, level_ref),
        (coupling_in, coupling_ref),
    )
    for copy in copies(pairs, sems):
        copy.wait()
    count = mass_ref.shape[1]
    local = wave_ref[...] - place_ref[0] * OWN
    index = lax.broadcasted_iota(jnp.int32, (OWN, count), 1)
    owner = lax.broadcasted_iota(jnp.int32, (OWN, count), 0) == local
    first_at = jnp.min(jnp.where(owner, index, count), axis=1, keepdims=True)
    first = owner & (index == first_at)
    second = owner & (index != first_at)
    mass = mass_ref[...]
    square = mass * mass
    inverse = 1.0 / (mass * width_ref[...])
    columns = [
        jnp.sum(jnp.where(mask, value, 0.0), axis=1, keepdims=True)
        for mask in (first, second)
        for value in (square, inverse)
    ]
    lane = lax.broadcasted_iota(jnp.int32, (OWN, LANES), 1)
    table = jnp.zeros((OWN, LANES), jnp.float32)
    for place, column in enumerate(columns):
        table = jnp.where(lane == place, column, table)
    turned = jnp.concatenate([table, jnp.zeros((LANES - OWN, LANES), jnp.float32)], axis=0).T
    rest = jnp.concatenate(
        [level_ref[...].astype(jnp.float32), coupling_ref[...], jnp.zeros((1, OWN), jnp.float32)], axis=0
    )
    rows = jnp.concatenate([turned[0:4, 0:OWN], rest], axis=1)
    send_terms(rows, out_ref)


def load_table(table_ref, wide_ref, chooser_ref):
    blocks = table_ref.shape[0]
    levels = chooser_ref.shape[1]
    stacked = [table_ref[block] for block in range(blocks)]
    stacked.append(jnp.zeros((LANES - 4 * blocks, LANES), jnp.float32))
    turned = jnp.concatenate(stacked, axis=0).T
    column = lax.broadcasted_iota(jnp.int32, (OWN, levels), 1).astype(jnp.float32)
    for block in range(blocks):
        rows = slice(block * OWN, (block + 1) * OWN)
        for pair in range(2):
            first = 4 * block + 2 * pair
            square = turned[0:OWN, first : first + 1]
            inverse = turned[0:OWN, first + 1 : first + 2]
            wide_ref[2 * pair, rows, :] = jnp.broadcast_to(square, (OWN, LANES))
            wide_ref[2 * pair + 1, rows, :] = jnp.broadcast_to(inverse, (OWN, LANES))
        level = turned[OWN : 2 * OWN, 4 * block : 4 * block + 1]
        chooser_ref[rows, :] = (level == column).astype(jnp.bfloat16)


def lineshapes(mass, wide_ref, rows):
    real = imag = None
    for pair in range(2):
        gap = (wide_ref[2 * pair, rows, :] - mass) * wide_ref[2 * pair + 1, rows, :]
        share = 1.0 / (gap * gap + 1.0)
        real = gap * share if real is None else real + gap * share
        imag = share if imag is None else imag + share
    return real, imag


def fill_tile(mass_row, basis_tile, wide_ref, chooser_ref, store):
    waves = chooser_ref.shape[0]
    masses = [
        jnp.broadcast_to(mass_row[:, half : half + LANES], (ROWS, LANES)) for half in range(0, TILE, LANES)
    ]
    for start in range(0, waves, OWN):
        angular = jnp.dot(chooser_ref[start : start + OWN, :], basis_tile, preferred_element_type=jnp.float32)
        for inner in range(0, OWN, ROWS):
            rows = slice(start + inner, start + inner + ROWS)
            reals, imags = [], []
            for half, mass in enumerate(masses):
                real, imag = lineshapes(mass, wide_ref, rows)
                scale = angular[inner : inner + ROWS, half * LANES : (half + 1) * LANES]
                reals.append(real * scale)
                imags.append(imag * scale)
            real = jnp.concatenate(reals, axis=1).astype(jnp.bfloat16)
            imag = jnp.concatenate(imags, axis=1).astype(jnp.bfloat16)
            store(2 * start + inner, real, imag)


def gram_kernel(
    scale, table_ref, mass_in, basis_in, data_mass_in, data_basis_in, weight_in, place_ref,
    out_ref, wide_ref, chooser_ref, data_mass_ref, data_basis_ref, weight_ref,
    mass_ref, basis_ref, amp_ref, sum_ref, turn_ref, sems, data_sems
):
    now = copies(((mass_in, mass_ref), (basis_in, basis_ref)), sems)
    later = copies(
        ((data_mass_in, data_mass_ref), (data_basis_in, data_basis_ref), (weight_in, weight_ref)), data_sems
    )
    load_table(table_ref, wide_ref, chooser_ref)
    sum_ref[...] = jnp.zeros_like(sum_ref)
    blocks = table_ref.shape[0]

    def store(row, real, imag):
        amp_ref[row : row + ROWS, :] = real
        amp_ref[row + OWN : row + OWN + ROWS, :] = imag

    for copy in now:
        copy.wait()

    @pl.loop(0, mass_ref.shape[1] // TILE)
    def _(step):
        columns = pl.ds(pl.multiple_of(step * TILE, TILE), TILE)
        fill_tile(mass_ref[:, columns], basis_ref[:, columns], wide_ref, chooser_ref, store)
        own = amp_ref[pl.ds(pl.multiple_of(place_ref[0] * 2 * OWN, 2 * OWN), 2 * OWN), :]
        sum_ref[...] += lax.dot_general(
            amp_ref[...], own, (((1,), (1,)), ((), ())), preferred_element_type=jnp.float32
        )

    for block in range(blocks):
        real_rows = sum_ref[2 * block * OWN : (2 * block + 1) * OWN, :]
        imag_rows = sum_ref[(2 * block + 1) * OWN : (2 * block + 2) * OWN, :]
        gram_real = real_rows + pltpu.roll(imag_rows, OWN, 1)
        gram_imag = imag_rows - pltpu.roll(real_rows, OWN, 1)
        turned = (jnp.concatenate([gram_real, gram_imag], axis=0) * scale).T
        turn_ref[:, block, :] = turned[0:OWN, :]
    out_ref[...] = turn_ref[...].astype(jnp.bfloat16)
    for copy in later:
        copy.wait()


def load_coupling(coupling, parts_ref):
    blocks = coupling.shape[0]
    signed, swapped = signs(coupling)
    parts_ref[...] = jnp.zeros_like(parts_ref)
    for row, value in enumerate((signed, swapped)):
        high = value.astype(jnp.bfloat16)
        rest = value - high.astype(jnp.float32)
        middle = rest.astype(jnp.bfloat16)
        low = (rest - middle.astype(jnp.float32)).astype(jnp.bfloat16)
        for place, part in enumerate((high, middle, low)):
            wide = part.astype(jnp.float32)
            for block in range(blocks):
                parts_ref[2 * place + row : 2 * place + row + 1, block * LANES : (block + 1) * LANES] = wide[block : block + 1]
    return signed, swapped


def load_columns(signed, swapped, vector_rows, column_ref):
    blocks = vector_rows // LANES
    first = signed.shape[0] - blocks
    rows = [signed[first:], swapped[first:], jnp.zeros((LANES - 2 * blocks, LANES), jnp.float32)]
    turned = jnp.concatenate(rows, axis=0).T
    for place in range(2):
        for block in range(blocks):
            column = turned[:, place * blocks + block : place * blocks + block + 1]
            column_ref[place, block * LANES : (block + 1) * LANES, :] = jnp.broadcast_to(column, (LANES, LANES))


def field_of(parts, amp_ref, columns, column_ref=None):
    waves = amp_ref.shape[0]
    vector_rows = 0 if column_ref is None else column_ref.shape[1]
    matrix_rows = waves - vector_rows
    sums = jnp.dot(parts[:, :matrix_rows], amp_ref[:matrix_rows, columns], preferred_element_type=jnp.float32)
    real = (sums[4:5] + sums[2:3]) + sums[0:1]
    imag = (sums[5:6] + sums[3:4]) + sums[1:2]
    if vector_rows:
        lanes = TILE // LANES
        reals = [jnp.zeros((ROWS, LANES), jnp.float32) for _ in range(lanes)]
        imags = [jnp.zeros((ROWS, LANES), jnp.float32) for _ in range(lanes)]
        for start in range(0, vector_rows, ROWS):
            rows = slice(start, start + ROWS)
            values = amp_ref[matrix_rows + start : matrix_rows + start + ROWS, columns].astype(jnp.float32)
            by_real, by_imag = column_ref[0, rows, :], column_ref[1, rows, :]
            for place in range(lanes):
                value = values[:, place * LANES : (place + 1) * LANES]
                reals[place] = reals[place] + value * by_real
                imags[place] = imags[place] + value * by_imag
        real = real + jnp.sum(jnp.concatenate(reals, axis=1), axis=0, keepdims=True)
        imag = imag + jnp.sum(jnp.concatenate(imags, axis=1), axis=0, keepdims=True)
    return real, imag


def tile_at(step):
    if isinstance(step, int):
        return pl.ds(step * TILE, TILE)
    return pl.ds(pl.multiple_of(step * TILE, TILE), TILE)


def project_tile(real, imag, weight, own_tile, by_real_ref, by_imag_ref, curve_ref):
    power = real * real + imag * imag
    inverse = 1.0 / (power + BACKGROUND)
    weighting = weight * inverse
    real = real * weighting
    imag = imag * weighting
    curving = weighting * power * inverse
    for start in range(0, own_tile.shape[0], CHUNK):
        rows = slice(start, start + CHUNK)
        by_real = by_real_ref[rows, :]
        by_imag = by_imag_ref[rows, :]
        curve = curve_ref[rows, :]
        for half in range(0, own_tile.shape[1], LANES):
            lanes = slice(half, half + LANES)
            value = own_tile[rows, lanes].astype(jnp.float32)
            by_real = by_real + value * real[:, lanes]
            by_imag = by_imag + value * imag[:, lanes]
            curve = curve + value * value * curving[:, lanes]
        by_real_ref[rows, :] = by_real
        by_imag_ref[rows, :] = by_imag
        curve_ref[rows, :] = curve


def gradient_rows(scale, by_real_ref, by_imag_ref, curve_ref):
    low, high = slice(0, OWN), slice(OWN, 2 * OWN)
    grad = jnp.concatenate(
        [-(by_real_ref[low, :] + by_imag_ref[high, :]), by_real_ref[high, :] - by_imag_ref[low, :]], axis=0
    )
    curve = jnp.concatenate([curve_ref[low, :] + curve_ref[high, :], jnp.zeros((OWN, LANES), jnp.float32)], axis=0)
    grad_row = jnp.sum(grad.T, axis=0, keepdims=True) * scale
    curve_row = jnp.sum(curve.T, axis=0, keepdims=True) * scale
    return jnp.concatenate([grad_row, curve_row], axis=0)


def gram_rows(gram, signed, swapped, place_ref):
    mixed_real = jnp.sum(gram * signed, keepdims=True)
    mixed_imag = jnp.sum(gram * swapped, keepdims=True)
    row_weight = jnp.sum(jnp.abs(gram), keepdims=True)
    lane = lax.broadcasted_iota(jnp.int32, (1, LANES), 1)
    here = place_ref[1]
    grad_row = jnp.where(lane == here, mixed_real, 0.0) + jnp.where(lane == here + OWN, mixed_imag, 0.0)
    curve_row = jnp.where(lane == here + OWN, row_weight, 0.0)
    return jnp.concatenate([grad_row, curve_row], axis=0)


def signs(coupling):
    lane = lax.broadcasted_iota(jnp.int32, coupling.shape, 1)
    return jnp.where(lane < OWN, coupling, -coupling), pltpu.roll(coupling, OWN, 1)


def send_terms(terms, out_ref):
    for peer in range(out_ref.shape[0]):
        out_ref[peer] = terms


def merge_kernel(received_ref, out_ref):
    send_terms(jnp.sum(received_ref[...], axis=0), out_ref)


def clear(*refs):
    for ref in refs:
        ref[...] = jnp.zeros_like(ref)


def own_rows(place_ref):
    return pl.ds(pl.multiple_of(place_ref[0] * 2 * OWN, 2 * OWN), 2 * OWN)


def first_kernel(
    scale, table_ref, wide_ref, chooser_ref, mass_ref, basis_ref, weight_ref, place_ref,
    out_ref, coupling_ref, amp_out, amp_ref, parts_ref, by_real_ref, by_imag_ref, curve_ref, sems
):
    for block in range(table_ref.shape[0]):
        half = table_ref[block]
        coupling_ref[block : block + 1, :] = jnp.concatenate([half[1:2, OWN:LANES], half[2:3, OWN:LANES]], axis=1)
    load_coupling(coupling_ref[...], parts_ref)
    parts = parts_ref[...].astype(jnp.bfloat16)
    clear(by_real_ref, by_imag_ref, curve_ref)

    @pl.loop(0, mass_ref.shape[1] // TILE)
    def _(step):
        columns = pl.ds(pl.multiple_of(step * TILE, TILE), TILE)

        def store(row, real, imag):
            amp_ref[row : row + ROWS, columns] = real
            amp_ref[row + OWN : row + OWN + ROWS, columns] = imag

        fill_tile(mass_ref[:, columns], basis_ref[:, columns], wide_ref, chooser_ref, store)
        real, imag = field_of(parts, amp_ref, columns)
        own = amp_ref[own_rows(place_ref), columns]
        project_tile(real, imag, weight_ref[:, columns], own, by_real_ref, by_imag_ref, curve_ref)
        pltpu.make_async_copy(amp_ref.at[:, columns], amp_out.at[:, columns], sems.at[step]).start()

    out_ref[...] = gradient_rows(scale, by_real_ref, by_imag_ref, curve_ref)
    for step in range(amp_ref.shape[1] // TILE):
        columns = pl.ds(step * TILE, TILE)
        pltpu.make_async_copy(amp_ref.at[:, columns], amp_out.at[:, columns], sems.at[step]).wait()


def add_kernel(pieces_ref, base_ref, coupling_ref, place_ref, out_ref, gram_ref):
    gram = jnp.sum(pieces_ref[...].astype(jnp.float32), axis=0)
    gram_ref[...] = gram
    send_terms(base_ref[...] + gram_rows(gram, *signs(coupling_ref[...]), place_ref), out_ref)


def new_coupling(received_ref, coupling_ref):
    blocks = coupling_ref.shape[0]
    total = received_ref[0:blocks] + received_ref[blocks : 2 * blocks]
    grad = total[:, 0, :]
    curve = total[:, 1, :]
    return coupling_ref[...] - grad / (curve + pltpu.roll(curve, OWN, 1))


def next_pass(
    scale, received_ref, old_ref, amp_ref, arrive, weight_ref, place_ref, gram_ref, out_ref, coupling_ref,
    parts_ref, by_real_ref, by_imag_ref, curve_ref, column_ref
):
    coupling = new_coupling(received_ref, old_ref)
    coupling_ref[...] = coupling
    signed, swapped = load_coupling(coupling, parts_ref)
    load_columns(signed, swapped, column_ref.shape[1], column_ref)
    parts = parts_ref[...].astype(jnp.bfloat16)
    clear(by_real_ref, by_imag_ref, curve_ref)
    tiles = amp_ref.shape[1] // TILE

    def project(step, field):
        own = amp_ref[own_rows(place_ref), tile_at(step)]
        project_tile(*field, weight_ref[:, tile_at(step)], own, by_real_ref, by_imag_ref, curve_ref)

    def ahead(step, field):
        arrive(step + 1)
        later = field_of(parts, amp_ref, tile_at(step + 1), column_ref)
        project(step, field)
        return later

    arrive(0)
    field = lax.fori_loop(0, tiles - 1, ahead, field_of(parts, amp_ref, tile_at(0), column_ref))
    project(tiles - 1, field)
    terms = gradient_rows(scale, by_real_ref, by_imag_ref, curve_ref)
    send_terms(terms + gram_rows(gram_ref[...], signed, swapped, place_ref), out_ref)


def second_kernel(scale, received_ref, old_ref, amp_in, weight_ref, place_ref, gram_ref, out_ref, coupling_ref, amp_ref, *scratch):
    sems = scratch[-1]

    def copy(step):
        return pltpu.make_async_copy(amp_in.at[:, tile_at(step)], amp_ref.at[:, tile_at(step)], sems.at[step])

    for step in range(amp_ref.shape[1] // TILE):
        copy(step).start()
    next_pass(
        scale, received_ref, old_ref, amp_ref, lambda step: copy(step).wait(), weight_ref, place_ref, gram_ref,
        out_ref, coupling_ref, *scratch[:-1]
    )


def next_kernel(scale, received_ref, old_ref, amp_ref, weight_ref, place_ref, gram_ref, *rest):
    next_pass(
        scale, received_ref, old_ref, amp_ref, lambda step: None, weight_ref, place_ref, gram_ref, *rest
    )


def last_kernel(
    received_ref, old_ref, amp_ref, place_ref, coupling_out_ref, intensity_ref, parts_ref, coupling_ref, column_ref
):
    coupling = new_coupling(received_ref, old_ref)
    coupling_ref[...] = coupling
    signed, swapped = load_coupling(coupling, parts_ref)
    load_columns(signed, swapped, column_ref.shape[1], column_ref)
    parts = parts_ref[...].astype(jnp.bfloat16)
    mine = coupling_ref[pl.ds(place_ref[0], 1), :]
    coupling_out_ref[0:1, :] = mine[:, 0:OWN]
    coupling_out_ref[1:2, :] = pltpu.roll(mine, OWN, 1)[:, 0:OWN]

    @pl.loop(0, amp_ref.shape[1] // TILE)
    def _(step):
        real, imag = field_of(parts, amp_ref, tile_at(step), column_ref)
        intensity_ref[:, tile_at(step)] = real * real + imag * imag + BACKGROUND


def call(kernel, outs, scratch, *args, smem, hbm=(), hbm_out=(), cost=None):
    def space(place):
        return pltpu.SMEM if place in smem else pltpu.HBM if place in hbm else pltpu.VMEM

    single = not isinstance(outs, tuple)
    whole = pl.BlockSpec(memory_space=pltpu.VMEM)
    return pl.pallas_call(
        kernel,
        out_shape=outs,
        in_specs=[pl.BlockSpec(memory_space=space(place)) for place in range(len(args))],
        out_specs=whole
        if single
        else tuple(pl.BlockSpec(memory_space=pltpu.HBM) if place in hbm_out else whole for place in range(len(outs))),
        cost_estimate=cost,
        scratch_shapes=scratch,
        compiler_params=pltpu.CompilerParams(vmem_limit_bytes=VMEM_LIMIT),
    )(*(pltpu.with_memory_space_constraint(arg, pltpu.HBM) if place in hbm else arg for place, arg in enumerate(args)))


def shape(*dims, dtype=jnp.float32):
    return jax.ShapeDtypeStruct(dims, dtype)


def pass_scratch(waves):
    return [pltpu.VMEM((8, 2 * waves), jnp.float32)] + [pltpu.VMEM((2 * OWN, LANES), jnp.float32) for _ in range(3)]


def shards(
    mc_mass, mc_basis, data_mass, data_basis, data_weight, res_mass, res_width, res_wave, wave_q, couplings
):
    rows = lax.axis_size("wrow")
    waves = OWN * rows
    zx = lax.axis_size("z") * lax.axis_size("x")
    events = zx * lax.axis_size("core")
    levels = mc_basis.shape[0]
    mc_count, data_count = mc_mass.shape[0], data_mass.shape[0]
    places = jnp.stack([lax.axis_index("wrow"), lax.axis_index(EVENT)]).astype(jnp.int32)
    own_table = call(
        prepare_kernel,
        shape(rows, 4, LANES),
        [
            pltpu.VMEM((1, res_mass.shape[0]), jnp.float32),
            pltpu.VMEM((1, res_width.shape[0]), jnp.float32),
            pltpu.VMEM((1, res_wave.shape[0]), jnp.int32),
            pltpu.VMEM((1, OWN), jnp.int32),
            pltpu.VMEM((2, OWN), jnp.float32),
            pltpu.SemaphoreType.DMA((5,)),
        ],
        res_mass[None], res_width[None], res_wave[None], wave_q[None], couplings, places,
        smem=(5,),
        hbm=range(5),
    )
    table = lax.all_to_all(own_table, "wrow", 0, 0)
    tile, wide, chooser, data_mass, data_basis, weight = call(
        functools.partial(gram_kernel, 1.0 / (mc_count * events)),
        (
            shape(OWN, rows, LANES, dtype=jnp.bfloat16),
            shape(PARAMS, waves, LANES),
            shape(waves, levels, dtype=jnp.bfloat16),
            shape(1, data_count),
            shape(levels, data_count, dtype=jnp.bfloat16),
            shape(1, data_count),
        ),
        [
            pltpu.VMEM((1, mc_count), jnp.float32),
            pltpu.VMEM((levels, mc_count), jnp.bfloat16),
            pltpu.VMEM((2 * waves, TILE), jnp.bfloat16),
            pltpu.VMEM((2 * waves, LANES), jnp.float32),
            pltpu.VMEM((OWN, rows, LANES), jnp.float32),
            pltpu.SemaphoreType.DMA((2,)),
            pltpu.SemaphoreType.DMA((3,)),
        ],
        table, mc_mass[None], mc_basis, data_mass[None], data_basis, data_weight[None], places,
        smem=(6,),
        hbm=range(1, 6),
    )
    pieces = lax.all_to_all(tile, EVENT, 0, 0)
    inverse_count = 1.0 / (data_count * events)
    tile_sems = pltpu.SemaphoreType.DMA((data_count // TILE,))
    amp_shape = (2 * waves, data_count)
    base, coupling, amp = call(
        functools.partial(first_kernel, inverse_count),
        (shape(2, LANES), shape(rows, LANES), pltpu.HBM(amp_shape, jnp.bfloat16)),
        [pltpu.VMEM(amp_shape, jnp.bfloat16)] + pass_scratch(waves) + [tile_sems],
        table, wide, chooser, data_mass, data_basis, weight, places,
        smem=(6,),
        hbm_out=(2,),
        cost=pl.CostEstimate(
            flops=40 * waves * data_count, bytes_accessed=8 * waves * data_count, transcendentals=waves * data_count
        ),
    )
    terms, gram_row = call(
        add_kernel, (shape(zx, 2, LANES), shape(rows, LANES)), [], pieces, base, coupling, places, smem=(3,)
    )

    def exchange(values):
        merged = call(merge_kernel, shape(2 * rows, 2, LANES), [], lax.all_to_all(values, ZX, 0, 0), smem=())
        return lax.all_to_all(merged, PEERS, 0, 0)

    column_scratch = [pltpu.VMEM((2, NEXT_ROWS, LANES), jnp.float32)]
    for step in range(1, ITERS):
        received = exchange(terms)
        if step == 1:
            terms, coupling, amp = call(
                functools.partial(second_kernel, inverse_count),
                (shape(zx, 2, LANES), shape(rows, LANES), shape(*amp_shape, dtype=jnp.bfloat16)),
                pass_scratch(waves) + column_scratch + [tile_sems],
                received, coupling, amp, weight, places, gram_row,
                smem=(4,),
                hbm=(2,),
            )
        else:
            terms, coupling = call(
                functools.partial(next_kernel, inverse_count),
                (shape(zx, 2, LANES), shape(rows, LANES)),
                pass_scratch(waves) + column_scratch,
                received, coupling, amp, weight, places, gram_row,
                smem=(4,),
            )
    received = exchange(terms)
    coupling_out, intensity = call(
        last_kernel,
        (shape(2, OWN), shape(1, data_count)),
        [
            pltpu.VMEM((8, 2 * waves), jnp.float32),
            pltpu.VMEM((rows, LANES), jnp.float32),
            pltpu.VMEM((2, LAST_ROWS, LANES), jnp.float32),
        ],
        received, coupling, amp, places,
        smem=(3,),
    )
    return coupling_out, intensity.reshape(data_count)


def solution(mesh):
    chips = Mesh(mesh.devices.reshape(4, 8, 2, 8), ("z", "x", "core", "wrow"))
    placed = (
        P(EVENT),
        P(None, EVENT),
        P(EVENT),
        P(None, EVENT),
        P(EVENT),
        P("wrow"),
        P("wrow"),
        P("wrow"),
        P("wrow"),
        P(None, "wrow"),
    )
    return jax.shard_map(
        shards, mesh=chips, in_specs=placed, out_specs=(P(None, "wrow"), P(EVENT)), check_vma=False
    )
```

```python
import functools

import jax
import jax.numpy as jnp
from jax import lax
from jax.experimental import pallas as pl
from jax.experimental.pallas import tpu as pltpu
from jax.sharding import Mesh, PartitionSpec as P

ITERS = 3
BACKGROUND = 0.5
ZX = ("z", "x")
EVENT = ("z", "x", "core")
PEERS = ("core", "wrow")
OWN = 64
LANES = 128
TILE = 512
CHUNK = 16
ROWS = 8
PARAMS = 4
NEXT_ROWS = 256
LAST_ROWS = 256
HEAD = 1
VMEM_LIMIT = 24 << 20


def copies(pairs, sems):
    started = [pltpu.make_async_copy(source, target, sems.at[place]) for place, (source, target) in enumerate(pairs)]
    for copy in started:
        copy.start()
    return started


def prepare_kernel(
    mass_in, width_in, wave_in, level_in, coupling_in, mc_mass_in, mc_basis_in, place_ref,
    out_ref, mc_mass_ref, mc_basis_ref, mass_ref, width_ref, wave_ref, level_ref, coupling_ref, sems, mc_sems
):
    pairs = (
        (mass_in, mass_ref),
        (width_in, width_ref),
        (wave_in, wave_ref),
        (level_in, level_ref),
        (coupling_in, coupling_ref),
    )
    small = copies(pairs, sems)
    large = copies(((mc_mass_in, mc_mass_ref), (mc_basis_in, mc_basis_ref)), mc_sems)
    for copy in small:
        copy.wait()
    count = mass_ref.shape[1]
    local = wave_ref[...] - place_ref[0] * OWN
    index = lax.broadcasted_iota(jnp.int32, (OWN, count), 1)
    owner = lax.broadcasted_iota(jnp.int32, (OWN, count), 0) == local
    first_at = jnp.min(jnp.where(owner, index, count), axis=1, keepdims=True)
    first = owner & (index == first_at)
    second = owner & (index != first_at)
    mass = mass_ref[...]
    square = mass * mass
    inverse = 1.0 / (mass * width_ref[...])
    columns = [
        jnp.sum(jnp.where(mask, value, 0.0), axis=1, keepdims=True)
        for mask in (first, second)
        for value in (square, inverse)
    ]
    lane = lax.broadcasted_iota(jnp.int32, (OWN, LANES), 1)
    table = jnp.zeros((OWN, LANES), jnp.float32)
    for place, column in enumerate(columns):
        table = jnp.where(lane == place, column, table)
    turned = jnp.concatenate([table, jnp.zeros((LANES - OWN, LANES), jnp.float32)], axis=0).T
    rest = jnp.concatenate(
        [level_ref[...].astype(jnp.float32), coupling_ref[...], jnp.zeros((1, OWN), jnp.float32)], axis=0
    )
    rows = jnp.concatenate([turned[0:4, 0:OWN], rest], axis=1)
    send_terms(rows, out_ref)
    for copy in large:
        copy.wait()


def load_table(table_ref, wide_ref, chooser_ref):
    blocks = table_ref.shape[0]
    levels = chooser_ref.shape[1]
    stacked = [table_ref[block] for block in range(blocks)]
    stacked.append(jnp.zeros((LANES - 4 * blocks, LANES), jnp.float32))
    turned = jnp.concatenate(stacked, axis=0).T
    column = lax.broadcasted_iota(jnp.int32, (OWN, levels), 1).astype(jnp.float32)
    for block in range(blocks):
        rows = slice(block * OWN, (block + 1) * OWN)
        for pair in range(2):
            first = 4 * block + 2 * pair
            square = turned[0:OWN, first : first + 1]
            inverse = turned[0:OWN, first + 1 : first + 2]
            wide_ref[2 * pair, rows, :] = jnp.broadcast_to(square, (OWN, LANES))
            wide_ref[2 * pair + 1, rows, :] = jnp.broadcast_to(inverse, (OWN, LANES))
        level = turned[OWN : 2 * OWN, 4 * block : 4 * block + 1]
        chooser_ref[rows, :] = (level == column).astype(jnp.bfloat16)


def lineshapes(mass, wide_ref, rows):
    real = imag = None
    for pair in range(2):
        gap = (wide_ref[2 * pair, rows, :] - mass) * wide_ref[2 * pair + 1, rows, :]
        share = 1.0 / (gap * gap + 1.0)
        real = gap * share if real is None else real + gap * share
        imag = share if imag is None else imag + share
    return real, imag


def fill_tile(mass_row, basis_tile, wide_ref, chooser_ref, store):
    waves = chooser_ref.shape[0]
    masses = [
        jnp.broadcast_to(mass_row[:, half : half + LANES], (ROWS, LANES)) for half in range(0, TILE, LANES)
    ]
    for start in range(0, waves, OWN):
        angular = jnp.dot(chooser_ref[start : start + OWN, :], basis_tile, preferred_element_type=jnp.float32)
        for inner in range(0, OWN, ROWS):
            rows = slice(start + inner, start + inner + ROWS)
            reals, imags = [], []
            for half, mass in enumerate(masses):
                real, imag = lineshapes(mass, wide_ref, rows)
                scale = angular[inner : inner + ROWS, half * LANES : (half + 1) * LANES]
                reals.append(real * scale)
                imags.append(imag * scale)
            real = jnp.concatenate(reals, axis=1).astype(jnp.bfloat16)
            imag = jnp.concatenate(imags, axis=1).astype(jnp.bfloat16)
            store(2 * start + inner, real, imag)


def gram_kernel(
    scale, table_ref, mass_ref, basis_ref, data_mass_in, data_basis_in, weight_in, place_ref,
    out_ref, wide_ref, chooser_ref, data_mass_ref, data_basis_ref, weight_ref,
    amp_ref, sum_ref, turn_ref, data_sems
):
    later = copies(
        ((data_mass_in, data_mass_ref), (data_basis_in, data_basis_ref), (weight_in, weight_ref)), data_sems
    )
    load_table(table_ref, wide_ref, chooser_ref)
    sum_ref[...] = jnp.zeros_like(sum_ref)
    blocks = table_ref.shape[0]

    def store(row, real, imag):
        amp_ref[row : row + ROWS, :] = real
        amp_ref[row + OWN : row + OWN + ROWS, :] = imag

    @pl.loop(0, mass_ref.shape[1] // TILE)
    def _(step):
        columns = pl.ds(pl.multiple_of(step * TILE, TILE), TILE)
        fill_tile(mass_ref[:, columns], basis_ref[:, columns], wide_ref, chooser_ref, store)
        own = amp_ref[pl.ds(pl.multiple_of(place_ref[0] * 2 * OWN, 2 * OWN), 2 * OWN), :]
        sum_ref[...] += lax.dot_general(
            amp_ref[...], own, (((1,), (1,)), ((), ())), preferred_element_type=jnp.float32
        )

    for block in range(blocks):
        real_rows = sum_ref[2 * block * OWN : (2 * block + 1) * OWN, :]
        imag_rows = sum_ref[(2 * block + 1) * OWN : (2 * block + 2) * OWN, :]
        gram_real = real_rows + pltpu.roll(imag_rows, OWN, 1)
        gram_imag = imag_rows - pltpu.roll(real_rows, OWN, 1)
        turned = (jnp.concatenate([gram_real, gram_imag], axis=0) * scale).T
        turn_ref[:, block, :] = turned[0:OWN, :]
    out_ref[...] = turn_ref[...].astype(jnp.bfloat16)
    for copy in later:
        copy.wait()


def load_coupling(coupling, parts_ref):
    blocks = coupling.shape[0]
    signed, swapped = signs(coupling)
    parts_ref[...] = jnp.zeros_like(parts_ref)
    for row, value in enumerate((signed, swapped)):
        high = value.astype(jnp.bfloat16)
        rest = value - high.astype(jnp.float32)
        middle = rest.astype(jnp.bfloat16)
        low = (rest - middle.astype(jnp.float32)).astype(jnp.bfloat16)
        for place, part in enumerate((high, middle, low)):
            wide = part.astype(jnp.float32)
            for block in range(blocks):
                parts_ref[2 * place + row : 2 * place + row + 1, block * LANES : (block + 1) * LANES] = wide[block : block + 1]
    return signed, swapped


def load_columns(signed, swapped, vector_rows, column_ref):
    blocks = vector_rows // LANES
    first = signed.shape[0] - blocks
    rows = [signed[first:], swapped[first:], jnp.zeros((LANES - 2 * blocks, LANES), jnp.float32)]
    turned = jnp.concatenate(rows, axis=0).T
    for place in range(2):
        for block in range(blocks):
            column = turned[:, place * blocks + block : place * blocks + block + 1]
            column_ref[place, block * LANES : (block + 1) * LANES, :] = jnp.broadcast_to(column, (LANES, LANES))


def field_of(parts, amp_ref, columns, column_ref=None):
    waves = amp_ref.shape[0]
    vector_rows = 0 if column_ref is None else column_ref.shape[1]
    matrix_rows = waves - vector_rows
    sums = jnp.dot(parts[:, :matrix_rows], amp_ref[:matrix_rows, columns], preferred_element_type=jnp.float32)
    real = (sums[4:5] + sums[2:3]) + sums[0:1]
    imag = (sums[5:6] + sums[3:4]) + sums[1:2]
    if vector_rows:
        lanes = TILE // LANES
        reals = [jnp.zeros((ROWS, LANES), jnp.float32) for _ in range(lanes)]
        imags = [jnp.zeros((ROWS, LANES), jnp.float32) for _ in range(lanes)]
        for start in range(0, vector_rows, ROWS):
            rows = slice(start, start + ROWS)
            values = amp_ref[matrix_rows + start : matrix_rows + start + ROWS, columns].astype(jnp.float32)
            by_real, by_imag = column_ref[0, rows, :], column_ref[1, rows, :]
            for place in range(lanes):
                value = values[:, place * LANES : (place + 1) * LANES]
                reals[place] = reals[place] + value * by_real
                imags[place] = imags[place] + value * by_imag
        real = real + jnp.sum(jnp.concatenate(reals, axis=1), axis=0, keepdims=True)
        imag = imag + jnp.sum(jnp.concatenate(imags, axis=1), axis=0, keepdims=True)
    return real, imag


def tile_at(step):
    if isinstance(step, int):
        return pl.ds(step * TILE, TILE)
    return pl.ds(pl.multiple_of(step * TILE, TILE), TILE)


def project_tile(real, imag, weight, own_tile, by_real_ref, by_imag_ref, curve_ref):
    power = real * real + imag * imag
    inverse = 1.0 / (power + BACKGROUND)
    weighting = weight * inverse
    real = real * weighting
    imag = imag * weighting
    curving = weighting * power * inverse
    for start in range(0, own_tile.shape[0], CHUNK):
        rows = slice(start, start + CHUNK)
        by_real = by_real_ref[rows, :]
        by_imag = by_imag_ref[rows, :]
        curve = curve_ref[rows, :]
        for half in range(0, own_tile.shape[1], LANES):
            lanes = slice(half, half + LANES)
            value = own_tile[rows, lanes].astype(jnp.float32)
            by_real = by_real + value * real[:, lanes]
            by_imag = by_imag + value * imag[:, lanes]
            curve = curve + value * value * curving[:, lanes]
        by_real_ref[rows, :] = by_real
        by_imag_ref[rows, :] = by_imag
        curve_ref[rows, :] = curve


def gradient_rows(scale, by_real_ref, by_imag_ref, curve_ref):
    low, high = slice(0, OWN), slice(OWN, 2 * OWN)
    grad = jnp.concatenate(
        [-(by_real_ref[low, :] + by_imag_ref[high, :]), by_real_ref[high, :] - by_imag_ref[low, :]], axis=0
    )
    curve = jnp.concatenate([curve_ref[low, :] + curve_ref[high, :], jnp.zeros((OWN, LANES), jnp.float32)], axis=0)
    grad_row = jnp.sum(grad.T, axis=0, keepdims=True) * scale
    curve_row = jnp.sum(curve.T, axis=0, keepdims=True) * scale
    return jnp.concatenate([grad_row, curve_row], axis=0)


def gram_rows(gram, signed, swapped, place_ref):
    mixed_real = jnp.sum(gram * signed, keepdims=True)
    mixed_imag = jnp.sum(gram * swapped, keepdims=True)
    row_weight = jnp.sum(jnp.abs(gram), keepdims=True)
    lane = lax.broadcasted_iota(jnp.int32, (1, LANES), 1)
    here = place_ref[1]
    grad_row = jnp.where(lane == here, mixed_real, 0.0) + jnp.where(lane == here + OWN, mixed_imag, 0.0)
    curve_row = jnp.where(lane == here + OWN, row_weight, 0.0)
    return jnp.concatenate([grad_row, curve_row], axis=0)


def signs(coupling):
    lane = lax.broadcasted_iota(jnp.int32, coupling.shape, 1)
    return jnp.where(lane < OWN, coupling, -coupling), pltpu.roll(coupling, OWN, 1)


def send_terms(terms, out_ref):
    for peer in range(out_ref.shape[0]):
        out_ref[peer] = terms


def merge_kernel(received_ref, out_ref):
    send_terms(jnp.sum(received_ref[...], axis=0), out_ref)


def clear(*refs):
    for ref in refs:
        ref[...] = jnp.zeros_like(ref)


def own_rows(place_ref):
    return pl.ds(pl.multiple_of(place_ref[0] * 2 * OWN, 2 * OWN), 2 * OWN)


def first_kernel(
    scale, table_ref, wide_ref, chooser_ref, mass_ref, basis_ref, weight_ref, place_ref,
    out_ref, coupling_ref, head_ref, amp_out, amp_ref, parts_ref, by_real_ref, by_imag_ref, curve_ref, sems
):
    for block in range(table_ref.shape[0]):
        half = table_ref[block]
        coupling_ref[block : block + 1, :] = jnp.concatenate([half[1:2, OWN:LANES], half[2:3, OWN:LANES]], axis=1)
    load_coupling(coupling_ref[...], parts_ref)
    parts = parts_ref[...].astype(jnp.bfloat16)
    clear(by_real_ref, by_imag_ref, curve_ref)
    tail = amp_ref.shape[1] // TILE

    def compute(event_tile, target_ref, target_tile):
        events, columns = tile_at(event_tile), tile_at(target_tile)

        def store(row, real, imag):
            target_ref[row : row + ROWS, columns] = real
            target_ref[row + OWN : row + OWN + ROWS, columns] = imag

        fill_tile(mass_ref[:, events], basis_ref[:, events], wide_ref, chooser_ref, store)
        real, imag = field_of(parts, target_ref, columns)
        own = target_ref[own_rows(place_ref), columns]
        project_tile(real, imag, weight_ref[:, events], own, by_real_ref, by_imag_ref, curve_ref)

    def copy(step):
        return pltpu.make_async_copy(amp_ref.at[:, tile_at(step)], amp_out.at[:, tile_at(step)], sems.at[step])

    @pl.loop(0, tail)
    def _(step):
        compute(step + HEAD, amp_ref, step)
        copy(step).start()

    compute(0, head_ref, 0)
    out_ref[...] = gradient_rows(scale, by_real_ref, by_imag_ref, curve_ref)
    for step in range(tail):
        copy(step).wait()


def add_kernel(pieces_ref, base_ref, coupling_ref, place_ref, out_ref, gram_ref):
    gram = jnp.sum(pieces_ref[...].astype(jnp.float32), axis=0)
    gram_ref[...] = gram
    send_terms(base_ref[...] + gram_rows(gram, *signs(coupling_ref[...]), place_ref), out_ref)


def new_coupling(received_ref, coupling_ref):
    blocks = coupling_ref.shape[0]
    total = received_ref[0:blocks] + received_ref[blocks : 2 * blocks]
    grad = total[:, 0, :]
    curve = total[:, 1, :]
    return coupling_ref[...] - grad / (curve + pltpu.roll(curve, OWN, 1))


def next_pass(
    scale, received_ref, old_ref, head_ref, tail_ref, arrive, weight_ref, place_ref, gram_ref, out_ref, coupling_ref,
    parts_ref, by_real_ref, by_imag_ref, curve_ref, column_ref
):
    coupling = new_coupling(received_ref, old_ref)
    coupling_ref[...] = coupling
    signed, swapped = load_coupling(coupling, parts_ref)
    load_columns(signed, swapped, column_ref.shape[1], column_ref)
    parts = parts_ref[...].astype(jnp.bfloat16)
    clear(by_real_ref, by_imag_ref, curve_ref)
    tiles = tail_ref.shape[1] // TILE

    def field_at(source_ref, step):
        return field_of(parts, source_ref, tile_at(step), column_ref)

    def project(source_ref, step, event_tile, field):
        own = source_ref[own_rows(place_ref), tile_at(step)]
        project_tile(*field, weight_ref[:, tile_at(event_tile)], own, by_real_ref, by_imag_ref, curve_ref)

    def ahead(step, field):
        arrive(step + 1)
        later = field_at(tail_ref, step + 1)
        project(tail_ref, step, step + HEAD, field)
        return later

    field = field_at(head_ref, 0)
    arrive(0)
    later = field_at(tail_ref, 0)
    project(head_ref, 0, 0, field)
    field = lax.fori_loop(0, tiles - 1, ahead, later)
    project(tail_ref, tiles - 1, tiles - 1 + HEAD, field)
    terms = gradient_rows(scale, by_real_ref, by_imag_ref, curve_ref)
    send_terms(terms + gram_rows(gram_ref[...], signed, swapped, place_ref), out_ref)


def second_kernel(
    scale, received_ref, old_ref, head_ref, tail_in, weight_ref, place_ref, gram_ref, out_ref, coupling_ref, tail_ref, *scratch
):
    sems = scratch[-1]

    def copy(step):
        return pltpu.make_async_copy(tail_in.at[:, tile_at(step)], tail_ref.at[:, tile_at(step)], sems.at[step])

    for step in range(tail_ref.shape[1] // TILE):
        copy(step).start()
    next_pass(
        scale, received_ref, old_ref, head_ref, tail_ref, lambda step: copy(step).wait(), weight_ref, place_ref, gram_ref,
        out_ref, coupling_ref, *scratch[:-1]
    )


def next_kernel(scale, received_ref, old_ref, head_ref, tail_ref, *rest):
    next_pass(scale, received_ref, old_ref, head_ref, tail_ref, lambda step: None, *rest)


def last_kernel(
    received_ref, old_ref, head_ref, tail_ref, place_ref, coupling_out_ref, intensity_ref, parts_ref, coupling_ref, column_ref
):
    coupling = new_coupling(received_ref, old_ref)
    coupling_ref[...] = coupling
    signed, swapped = load_coupling(coupling, parts_ref)
    load_columns(signed, swapped, column_ref.shape[1], column_ref)
    parts = parts_ref[...].astype(jnp.bfloat16)
    mine = coupling_ref[pl.ds(place_ref[0], 1), :]
    coupling_out_ref[0:1, :] = mine[:, 0:OWN]
    coupling_out_ref[1:2, :] = pltpu.roll(mine, OWN, 1)[:, 0:OWN]

    def finish(source_ref, step, event_tile):
        real, imag = field_of(parts, source_ref, tile_at(step), column_ref)
        intensity_ref[:, tile_at(event_tile)] = real * real + imag * imag + BACKGROUND

    finish(head_ref, 0, 0)

    @pl.loop(0, tail_ref.shape[1] // TILE)
    def _(step):
        finish(tail_ref, step, step + HEAD)


def call(kernel, outs, scratch, *args, smem, hbm=(), hbm_out=(), cost=None):
    def space(place):
        return pltpu.SMEM if place in smem else pltpu.HBM if place in hbm else pltpu.VMEM

    single = not isinstance(outs, tuple)
    whole = pl.BlockSpec(memory_space=pltpu.VMEM)
    return pl.pallas_call(
        kernel,
        out_shape=outs,
        in_specs=[pl.BlockSpec(memory_space=space(place)) for place in range(len(args))],
        out_specs=whole
        if single
        else tuple(pl.BlockSpec(memory_space=pltpu.HBM) if place in hbm_out else whole for place in range(len(outs))),
        cost_estimate=cost,
        scratch_shapes=scratch,
        compiler_params=pltpu.CompilerParams(vmem_limit_bytes=VMEM_LIMIT),
    )(*(pltpu.with_memory_space_constraint(arg, pltpu.HBM) if place in hbm else arg for place, arg in enumerate(args)))


def shape(*dims, dtype=jnp.float32):
    return jax.ShapeDtypeStruct(dims, dtype)


def pass_scratch(waves):
    return [pltpu.VMEM((8, 2 * waves), jnp.float32)] + [pltpu.VMEM((2 * OWN, LANES), jnp.float32) for _ in range(3)]


def shards(
    mc_mass, mc_basis, data_mass, data_basis, data_weight, res_mass, res_width, res_wave, wave_q, couplings
):
    rows = lax.axis_size("wrow")
    waves = OWN * rows
    zx = lax.axis_size("z") * lax.axis_size("x")
    events = zx * lax.axis_size("core")
    levels = mc_basis.shape[0]
    mc_count, data_count = mc_mass.shape[0], data_mass.shape[0]
    places = jnp.stack([lax.axis_index("wrow"), lax.axis_index(EVENT)]).astype(jnp.int32)
    own_table, mc_mass, mc_basis = call(
        prepare_kernel,
        (shape(rows, 4, LANES), shape(1, mc_count), shape(levels, mc_count, dtype=jnp.bfloat16)),
        [
            pltpu.VMEM((1, res_mass.shape[0]), jnp.float32),
            pltpu.VMEM((1, res_width.shape[0]), jnp.float32),
            pltpu.VMEM((1, res_wave.shape[0]), jnp.int32),
            pltpu.VMEM((1, OWN), jnp.int32),
            pltpu.VMEM((2, OWN), jnp.float32),
            pltpu.SemaphoreType.DMA((5,)),
            pltpu.SemaphoreType.DMA((2,)),
        ],
        res_mass[None], res_width[None], res_wave[None], wave_q[None], couplings, mc_mass[None], mc_basis, places,
        smem=(7,),
        hbm=range(7),
    )
    table = lax.all_to_all(own_table, "wrow", 0, 0)
    tile, wide, chooser, data_mass, data_basis, weight = call(
        functools.partial(gram_kernel, 1.0 / (mc_count * events)),
        (
            shape(OWN, rows, LANES, dtype=jnp.bfloat16),
            shape(PARAMS, waves, LANES),
            shape(waves, levels, dtype=jnp.bfloat16),
            shape(1, data_count),
            shape(levels, data_count, dtype=jnp.bfloat16),
            shape(1, data_count),
        ),
        [
            pltpu.VMEM((2 * waves, TILE), jnp.bfloat16),
            pltpu.VMEM((2 * waves, LANES), jnp.float32),
            pltpu.VMEM((OWN, rows, LANES), jnp.float32),
            pltpu.SemaphoreType.DMA((3,)),
        ],
        table, mc_mass, mc_basis, data_mass[None], data_basis, data_weight[None], places,
        smem=(6,),
        hbm=range(3, 6),
    )
    pieces = lax.all_to_all(tile, EVENT, 0, 0)
    inverse_count = 1.0 / (data_count * events)
    tile_sems = pltpu.SemaphoreType.DMA((data_count // TILE,))
    tail_shape = (2 * waves, data_count - HEAD * TILE)
    base, coupling, head, tail = call(
        functools.partial(first_kernel, inverse_count),
        (
            shape(2, LANES),
            shape(rows, LANES),
            shape(2 * waves, HEAD * TILE, dtype=jnp.bfloat16),
            pltpu.HBM(tail_shape, jnp.bfloat16),
        ),
        [pltpu.VMEM(tail_shape, jnp.bfloat16)] + pass_scratch(waves) + [tile_sems],
        table, wide, chooser, data_mass, data_basis, weight, places,
        smem=(6,),
        hbm_out=(3,),
        cost=pl.CostEstimate(
            flops=40 * waves * data_count, bytes_accessed=8 * waves * data_count, transcendentals=waves * data_count
        ),
    )
    terms, gram_row = call(
        add_kernel, (shape(zx, 2, LANES), shape(rows, LANES)), [], pieces, base, coupling, places, smem=(3,)
    )

    def exchange(values):
        merged = call(merge_kernel, shape(2 * rows, 2, LANES), [], lax.all_to_all(values, ZX, 0, 0), smem=())
        return lax.all_to_all(merged, PEERS, 0, 0)

    column_scratch = [pltpu.VMEM((2, NEXT_ROWS, LANES), jnp.float32)]
    for step in range(1, ITERS):
        received = exchange(terms)
        if step == 1:
            terms, coupling, tail = call(
                functools.partial(second_kernel, inverse_count),
                (shape(zx, 2, LANES), shape(rows, LANES), shape(*tail_shape, dtype=jnp.bfloat16)),
                pass_scratch(waves) + column_scratch + [tile_sems],
                received, coupling, head, tail, weight, places, gram_row,
                smem=(5,),
                hbm=(3,),
            )
        else:
            terms, coupling = call(
                functools.partial(next_kernel, inverse_count),
                (shape(zx, 2, LANES), shape(rows, LANES)),
                pass_scratch(waves) + column_scratch,
                received, coupling, head, tail, weight, places, gram_row,
                smem=(5,),
            )
    received = exchange(terms)
    coupling_out, intensity = call(
        last_kernel,
        (shape(2, OWN), shape(1, data_count)),
        [
            pltpu.VMEM((8, 2 * waves), jnp.float32),
            pltpu.VMEM((rows, LANES), jnp.float32),
            pltpu.VMEM((2, LAST_ROWS, LANES), jnp.float32),
        ],
        received, coupling, head, tail, places,
        smem=(4,),
    )
    return coupling_out, intensity.reshape(data_count)


def solution(mesh):
    chips = Mesh(mesh.devices.reshape(4, 8, 2, 8), ("z", "x", "core", "wrow"))
    placed = (
        P(EVENT),
        P(None, EVENT),
        P(EVENT),
        P(None, EVENT),
        P(EVENT),
        P("wrow"),
        P("wrow"),
        P("wrow"),
        P("wrow"),
        P(None, "wrow"),
    )
    return jax.shard_map(
        shards, mesh=chips, in_specs=placed, out_specs=(P(None, "wrow"), P(EVENT)), check_vma=False
    )
```

```python
import functools

import jax
import jax.numpy as jnp
from jax import lax
from jax.experimental import pallas as pl
from jax.experimental.pallas import tpu as pltpu
from jax.sharding import Mesh, PartitionSpec as P

ITERS = 3
BACKGROUND = 0.5
ZX = ("z", "x")
EVENT = ("z", "x", "core")
PEERS = ("core", "wrow")
OWN = 64
LANES = 128
TILE = 512
CHUNK = 16
ROWS = 8
PARAMS = 4
NEXT_ROWS = 256
LAST_ROWS = 256
HEAD = 1
AHEAD = 3
VMEM_LIMIT = 24 << 20


def copies(pairs, sems):
    started = [pltpu.make_async_copy(source, target, sems.at[place]) for place, (source, target) in enumerate(pairs)]
    for copy in started:
        copy.start()
    return started


def prepare_kernel(
    mass_in, width_in, wave_in, level_in, coupling_in, mc_mass_in, mc_basis_in,
    out_ref, mc_mass_ref, mc_basis_ref, mass_ref, width_ref, wave_ref, level_ref, coupling_ref, sems, mc_sems
):
    place_ref = here()
    pairs = (
        (mass_in, mass_ref),
        (width_in, width_ref),
        (wave_in, wave_ref),
        (level_in, level_ref),
        (coupling_in, coupling_ref),
    )
    small = copies(pairs, sems)
    large = copies(((mc_mass_in, mc_mass_ref), (mc_basis_in, mc_basis_ref)), mc_sems)
    for copy in small:
        copy.wait()
    count = mass_ref.shape[1]
    local = wave_ref[...] - place_ref[0] * OWN
    index = lax.broadcasted_iota(jnp.int32, (OWN, count), 1)
    owner = lax.broadcasted_iota(jnp.int32, (OWN, count), 0) == local
    first_at = jnp.min(jnp.where(owner, index, count), axis=1, keepdims=True)
    first = owner & (index == first_at)
    second = owner & (index != first_at)
    mass = mass_ref[...]
    square = mass * mass
    inverse = 1.0 / (mass * width_ref[...])
    columns = [
        jnp.sum(jnp.where(mask, value, 0.0), axis=1, keepdims=True)
        for mask in (first, second)
        for value in (square, inverse)
    ]
    lane = lax.broadcasted_iota(jnp.int32, (OWN, LANES), 1)
    table = jnp.zeros((OWN, LANES), jnp.float32)
    for place, column in enumerate(columns):
        table = jnp.where(lane == place, column, table)
    turned = jnp.concatenate([table, jnp.zeros((LANES - OWN, LANES), jnp.float32)], axis=0).T
    rest = jnp.concatenate(
        [level_ref[...].astype(jnp.float32), coupling_ref[...], jnp.zeros((1, OWN), jnp.float32)], axis=0
    )
    rows = jnp.concatenate([turned[0:4, 0:OWN], rest], axis=1)
    send_terms(rows, out_ref)
    for copy in large:
        copy.wait()


def load_table(table_ref, wide_ref, chooser_ref):
    blocks = table_ref.shape[0]
    levels = chooser_ref.shape[1]
    stacked = [table_ref[block] for block in range(blocks)]
    stacked.append(jnp.zeros((LANES - 4 * blocks, LANES), jnp.float32))
    turned = jnp.concatenate(stacked, axis=0).T
    column = lax.broadcasted_iota(jnp.int32, (OWN, levels), 1).astype(jnp.float32)
    for block in range(blocks):
        rows = slice(block * OWN, (block + 1) * OWN)
        for pair in range(2):
            first = 4 * block + 2 * pair
            square = turned[0:OWN, first : first + 1]
            inverse = turned[0:OWN, first + 1 : first + 2]
            wide_ref[2 * pair, rows, :] = jnp.broadcast_to(square, (OWN, LANES))
            wide_ref[2 * pair + 1, rows, :] = jnp.broadcast_to(inverse, (OWN, LANES))
        level = turned[OWN : 2 * OWN, 4 * block : 4 * block + 1]
        chooser_ref[rows, :] = (level == column).astype(jnp.bfloat16)


def lineshapes(mass, wide_ref, rows):
    real = imag = None
    for pair in range(2):
        gap = (wide_ref[2 * pair, rows, :] - mass) * wide_ref[2 * pair + 1, rows, :]
        share = 1.0 / (gap * gap + 1.0)
        real = gap * share if real is None else real + gap * share
        imag = share if imag is None else imag + share
    return real, imag


def fill_tile(mass_row, basis_tile, wide_ref, chooser_ref, store):
    waves = chooser_ref.shape[0]
    masses = [
        jnp.broadcast_to(mass_row[:, half : half + LANES], (ROWS, LANES)) for half in range(0, TILE, LANES)
    ]
    for start in range(0, waves, OWN):
        angular = jnp.dot(chooser_ref[start : start + OWN, :], basis_tile, preferred_element_type=jnp.float32)
        for inner in range(0, OWN, ROWS):
            rows = slice(start + inner, start + inner + ROWS)
            reals, imags = [], []
            for half, mass in enumerate(masses):
                real, imag = lineshapes(mass, wide_ref, rows)
                scale = angular[inner : inner + ROWS, half * LANES : (half + 1) * LANES]
                reals.append(real * scale)
                imags.append(imag * scale)
            real = jnp.concatenate(reals, axis=1).astype(jnp.bfloat16)
            imag = jnp.concatenate(imags, axis=1).astype(jnp.bfloat16)
            store(2 * start + inner, real, imag)


def gram_kernel(
    scale, table_ref, mass_ref, basis_ref, data_mass_in, data_basis_in, weight_in,
    out_ref, wide_ref, chooser_ref, data_mass_ref, data_basis_ref, weight_ref,
    amp_ref, sum_ref, turn_ref, data_sems
):
    place_ref = here()
    later = copies(
        ((data_mass_in, data_mass_ref), (data_basis_in, data_basis_ref), (weight_in, weight_ref)), data_sems
    )
    load_table(table_ref, wide_ref, chooser_ref)
    sum_ref[...] = jnp.zeros_like(sum_ref)
    blocks = table_ref.shape[0]

    def store(row, real, imag):
        amp_ref[row : row + ROWS, :] = real
        amp_ref[row + OWN : row + OWN + ROWS, :] = imag

    @pl.loop(0, mass_ref.shape[1] // TILE)
    def _(step):
        columns = pl.ds(pl.multiple_of(step * TILE, TILE), TILE)
        fill_tile(mass_ref[:, columns], basis_ref[:, columns], wide_ref, chooser_ref, store)
        own = amp_ref[pl.ds(pl.multiple_of(place_ref[0] * 2 * OWN, 2 * OWN), 2 * OWN), :]
        sum_ref[...] += lax.dot_general(
            amp_ref[...], own, (((1,), (1,)), ((), ())), preferred_element_type=jnp.float32
        )

    for block in range(blocks):
        real_rows = sum_ref[2 * block * OWN : (2 * block + 1) * OWN, :]
        imag_rows = sum_ref[(2 * block + 1) * OWN : (2 * block + 2) * OWN, :]
        gram_real = real_rows + pltpu.roll(imag_rows, OWN, 1)
        gram_imag = imag_rows - pltpu.roll(real_rows, OWN, 1)
        turned = (jnp.concatenate([gram_real, gram_imag], axis=0) * scale).T
        turn_ref[:, block, :] = turned[0:OWN, :]
    out_ref[...] = turn_ref[...].astype(jnp.bfloat16)
    for copy in later:
        copy.wait()


def load_coupling(coupling, parts_ref):
    blocks = coupling.shape[0]
    signed, swapped = signs(coupling)
    parts_ref[...] = jnp.zeros_like(parts_ref)
    for row, value in enumerate((signed, swapped)):
        high = value.astype(jnp.bfloat16)
        rest = value - high.astype(jnp.float32)
        middle = rest.astype(jnp.bfloat16)
        low = (rest - middle.astype(jnp.float32)).astype(jnp.bfloat16)
        for place, part in enumerate((high, middle, low)):
            wide = part.astype(jnp.float32)
            for block in range(blocks):
                parts_ref[2 * place + row : 2 * place + row + 1, block * LANES : (block + 1) * LANES] = wide[block : block + 1]
    return signed, swapped


def load_columns(signed, swapped, vector_rows, column_ref):
    blocks = vector_rows // LANES
    first = signed.shape[0] - blocks
    rows = [signed[first:], swapped[first:], jnp.zeros((LANES - 2 * blocks, LANES), jnp.float32)]
    turned = jnp.concatenate(rows, axis=0).T
    for place in range(2):
        for block in range(blocks):
            column = turned[:, place * blocks + block : place * blocks + block + 1]
            column_ref[place, block * LANES : (block + 1) * LANES, :] = jnp.broadcast_to(column, (LANES, LANES))


def field_of(parts, amp_ref, columns, column_ref=None):
    waves = amp_ref.shape[0]
    vector_rows = 0 if column_ref is None else column_ref.shape[1]
    matrix_rows = waves - vector_rows
    sums = jnp.dot(parts[:, :matrix_rows], amp_ref[:matrix_rows, columns], preferred_element_type=jnp.float32)
    real = (sums[4:5] + sums[2:3]) + sums[0:1]
    imag = (sums[5:6] + sums[3:4]) + sums[1:2]
    if vector_rows:
        lanes = TILE // LANES
        reals = [jnp.zeros((ROWS, LANES), jnp.float32) for _ in range(lanes)]
        imags = [jnp.zeros((ROWS, LANES), jnp.float32) for _ in range(lanes)]
        for start in range(0, vector_rows, ROWS):
            rows = slice(start, start + ROWS)
            values = amp_ref[matrix_rows + start : matrix_rows + start + ROWS, columns].astype(jnp.float32)
            by_real, by_imag = column_ref[0, rows, :], column_ref[1, rows, :]
            for place in range(lanes):
                value = values[:, place * LANES : (place + 1) * LANES]
                reals[place] = reals[place] + value * by_real
                imags[place] = imags[place] + value * by_imag
        real = real + jnp.sum(jnp.concatenate(reals, axis=1), axis=0, keepdims=True)
        imag = imag + jnp.sum(jnp.concatenate(imags, axis=1), axis=0, keepdims=True)
    return real, imag


def tile_at(step):
    if isinstance(step, int):
        return pl.ds(step * TILE, TILE)
    return pl.ds(pl.multiple_of(step * TILE, TILE), TILE)


def project_tile(real, imag, weight, own_tile, by_real_ref, by_imag_ref, curve_ref):
    power = real * real + imag * imag
    inverse = 1.0 / (power + BACKGROUND)
    weighting = weight * inverse
    real = real * weighting
    imag = imag * weighting
    curving = weighting * power * inverse
    for start in range(0, own_tile.shape[0], CHUNK):
        rows = slice(start, start + CHUNK)
        by_real = by_real_ref[rows, :]
        by_imag = by_imag_ref[rows, :]
        curve = curve_ref[rows, :]
        for half in range(0, own_tile.shape[1], LANES):
            lanes = slice(half, half + LANES)
            value = own_tile[rows, lanes].astype(jnp.float32)
            by_real = by_real + value * real[:, lanes]
            by_imag = by_imag + value * imag[:, lanes]
            curve = curve + value * value * curving[:, lanes]
        by_real_ref[rows, :] = by_real
        by_imag_ref[rows, :] = by_imag
        curve_ref[rows, :] = curve


def gradient_rows(scale, by_real_ref, by_imag_ref, curve_ref):
    low, high = slice(0, OWN), slice(OWN, 2 * OWN)
    grad = jnp.concatenate(
        [-(by_real_ref[low, :] + by_imag_ref[high, :]), by_real_ref[high, :] - by_imag_ref[low, :]], axis=0
    )
    curve = jnp.concatenate([curve_ref[low, :] + curve_ref[high, :], jnp.zeros((OWN, LANES), jnp.float32)], axis=0)
    grad_row = jnp.sum(grad.T, axis=0, keepdims=True) * scale
    curve_row = jnp.sum(curve.T, axis=0, keepdims=True) * scale
    return jnp.concatenate([grad_row, curve_row], axis=0)


def gram_rows(gram, signed, swapped, place_ref):
    mixed_real = jnp.sum(gram * signed, keepdims=True)
    mixed_imag = jnp.sum(gram * swapped, keepdims=True)
    row_weight = jnp.sum(jnp.abs(gram), keepdims=True)
    lane = lax.broadcasted_iota(jnp.int32, (1, LANES), 1)
    event = place_ref[1]
    grad_row = jnp.where(lane == event, mixed_real, 0.0) + jnp.where(lane == event + OWN, mixed_imag, 0.0)
    curve_row = jnp.where(lane == event + OWN, row_weight, 0.0)
    return jnp.concatenate([grad_row, curve_row], axis=0)


def signs(coupling):
    lane = lax.broadcasted_iota(jnp.int32, coupling.shape, 1)
    return jnp.where(lane < OWN, coupling, -coupling), pltpu.roll(coupling, OWN, 1)


def here():
    chip = lax.axis_index("z") * lax.axis_size("x") + lax.axis_index("x")
    return lax.axis_index("wrow"), chip * lax.axis_size("core") + lax.axis_index("core")


def send_terms(terms, out_ref):
    for peer in range(out_ref.shape[0]):
        out_ref[peer] = terms


def merge_kernel(received_ref, out_ref):
    send_terms(jnp.sum(received_ref[...], axis=0), out_ref)


def clear(*refs):
    for ref in refs:
        ref[...] = jnp.zeros_like(ref)


def own_rows(place_ref):
    return pl.ds(pl.multiple_of(place_ref[0] * 2 * OWN, 2 * OWN), 2 * OWN)


def first_kernel(
    scale, table_ref, wide_ref, chooser_ref, mass_ref, basis_ref, weight_ref,
    out_ref, coupling_ref, head_ref, amp_out, amp_ref, parts_ref, by_real_ref, by_imag_ref, curve_ref, sems
):
    place_ref = here()
    for block in range(table_ref.shape[0]):
        half = table_ref[block]
        coupling_ref[block : block + 1, :] = jnp.concatenate([half[1:2, OWN:LANES], half[2:3, OWN:LANES]], axis=1)
    load_coupling(coupling_ref[...], parts_ref)
    parts = parts_ref[...].astype(jnp.bfloat16)
    clear(by_real_ref, by_imag_ref, curve_ref)
    tail = amp_ref.shape[1] // TILE

    def compute(event_tile, target_ref, target_tile):
        events, columns = tile_at(event_tile), tile_at(target_tile)

        def store(row, real, imag):
            target_ref[row : row + ROWS, columns] = real
            target_ref[row + OWN : row + OWN + ROWS, columns] = imag

        fill_tile(mass_ref[:, events], basis_ref[:, events], wide_ref, chooser_ref, store)
        real, imag = field_of(parts, target_ref, columns)
        own = target_ref[own_rows(place_ref), columns]
        project_tile(real, imag, weight_ref[:, events], own, by_real_ref, by_imag_ref, curve_ref)

    def copy(step):
        return pltpu.make_async_copy(amp_ref.at[:, tile_at(step)], amp_out.at[:, tile_at(step)], sems.at[step])

    @pl.loop(0, tail)
    def _(step):
        compute(step + HEAD, amp_ref, step)
        copy(step).start()

    compute(0, head_ref, 0)
    out_ref[...] = gradient_rows(scale, by_real_ref, by_imag_ref, curve_ref)
    for step in range(tail):
        copy(step).wait()


def add_kernel(pieces_ref, base_ref, coupling_ref, out_ref, gram_ref):
    place_ref = here()
    gram = jnp.sum(pieces_ref[...].astype(jnp.float32), axis=0)
    gram_ref[...] = gram
    send_terms(base_ref[...] + gram_rows(gram, *signs(coupling_ref[...]), place_ref), out_ref)


def new_coupling(received_ref, coupling_ref):
    blocks = coupling_ref.shape[0]
    total = received_ref[0:blocks] + received_ref[blocks : 2 * blocks]
    grad = total[:, 0, :]
    curve = total[:, 1, :]
    return coupling_ref[...] - grad / (curve + pltpu.roll(curve, OWN, 1))


def next_pass(
    scale, received_ref, old_ref, head_ref, tail_ref, arrive, weight_ref, gram_ref, out_ref, coupling_ref,
    parts_ref, by_real_ref, by_imag_ref, curve_ref, column_ref
):
    place_ref = here()
    coupling = new_coupling(received_ref, old_ref)
    coupling_ref[...] = coupling
    signed, swapped = load_coupling(coupling, parts_ref)
    load_columns(signed, swapped, column_ref.shape[1], column_ref)
    parts = parts_ref[...].astype(jnp.bfloat16)
    clear(by_real_ref, by_imag_ref, curve_ref)
    tiles = tail_ref.shape[1] // TILE

    def field_at(source_ref, step):
        return field_of(parts, source_ref, tile_at(step), column_ref)

    def project(source_ref, step, event_tile, field):
        own = source_ref[own_rows(place_ref), tile_at(step)]
        project_tile(*field, weight_ref[:, tile_at(event_tile)], own, by_real_ref, by_imag_ref, curve_ref)

    def ahead(step, field):
        arrive(step + 1)
        later = field_at(tail_ref, step + 1)
        project(tail_ref, step, step + HEAD, field)
        return later

    field = field_at(head_ref, 0)
    arrive(0)
    later = field_at(tail_ref, 0)
    project(head_ref, 0, 0, field)
    field = lax.fori_loop(0, tiles - 1, ahead, later)
    project(tail_ref, tiles - 1, tiles - 1 + HEAD, field)
    terms = gradient_rows(scale, by_real_ref, by_imag_ref, curve_ref)
    send_terms(terms + gram_rows(gram_ref[...], signed, swapped, place_ref), out_ref)


def second_kernel(
    scale, received_ref, old_ref, head_ref, tail_in, weight_ref, gram_ref, out_ref, coupling_ref, tail_ref, *scratch
):
    sems = scratch[-1]

    def copy(step):
        return pltpu.make_async_copy(tail_in.at[:, tile_at(step)], tail_ref.at[:, tile_at(step)], sems.at[step])

    tiles = tail_ref.shape[1] // TILE

    def arrive(step):
        copy(step).wait()

        @pl.when(step + AHEAD < tiles)
        def _():
            copy(step + AHEAD).start()

    for step in range(AHEAD):
        copy(step).start()
    next_pass(
        scale, received_ref, old_ref, head_ref, tail_ref, arrive, weight_ref, gram_ref,
        out_ref, coupling_ref, *scratch[:-1]
    )


def next_kernel(scale, received_ref, old_ref, head_ref, tail_ref, *rest):
    next_pass(scale, received_ref, old_ref, head_ref, tail_ref, lambda step: None, *rest)


def last_kernel(
    received_ref, old_ref, head_ref, tail_ref, coupling_out_ref, intensity_ref, parts_ref, coupling_ref, column_ref
):
    place_ref = here()
    coupling = new_coupling(received_ref, old_ref)
    coupling_ref[...] = coupling
    signed, swapped = load_coupling(coupling, parts_ref)
    load_columns(signed, swapped, column_ref.shape[1], column_ref)
    parts = parts_ref[...].astype(jnp.bfloat16)
    mine = coupling_ref[pl.ds(place_ref[0], 1), :]
    coupling_out_ref[0:1, :] = mine[:, 0:OWN]
    coupling_out_ref[1:2, :] = pltpu.roll(mine, OWN, 1)[:, 0:OWN]

    def finish(source_ref, step, event_tile):
        real, imag = field_of(parts, source_ref, tile_at(step), column_ref)
        intensity_ref[:, tile_at(event_tile)] = real * real + imag * imag + BACKGROUND

    finish(head_ref, 0, 0)

    @pl.loop(0, tail_ref.shape[1] // TILE)
    def _(step):
        finish(tail_ref, step, step + HEAD)


def call(kernel, outs, scratch, *args, hbm=(), hbm_out=(), cost=None):
    def space(place):
        return pltpu.HBM if place in hbm else pltpu.VMEM

    single = not isinstance(outs, tuple)
    whole = pl.BlockSpec(memory_space=pltpu.VMEM)
    return pl.pallas_call(
        kernel,
        out_shape=outs,
        in_specs=[pl.BlockSpec(memory_space=space(place)) for place in range(len(args))],
        out_specs=whole
        if single
        else tuple(pl.BlockSpec(memory_space=pltpu.HBM) if place in hbm_out else whole for place in range(len(outs))),
        cost_estimate=cost,
        scratch_shapes=scratch,
        compiler_params=pltpu.CompilerParams(vmem_limit_bytes=VMEM_LIMIT),
    )(*(pltpu.with_memory_space_constraint(arg, pltpu.HBM) if place in hbm else arg for place, arg in enumerate(args)))


def shape(*dims, dtype=jnp.float32):
    return jax.ShapeDtypeStruct(dims, dtype)


def pass_scratch(waves):
    return [pltpu.VMEM((8, 2 * waves), jnp.float32)] + [pltpu.VMEM((2 * OWN, LANES), jnp.float32) for _ in range(3)]


def shards(
    mc_mass, mc_basis, data_mass, data_basis, data_weight, res_mass, res_width, res_wave, wave_q, couplings
):
    rows = lax.axis_size("wrow")
    waves = OWN * rows
    zx = lax.axis_size("z") * lax.axis_size("x")
    events = zx * lax.axis_size("core")
    levels = mc_basis.shape[0]
    mc_count, data_count = mc_mass.shape[0], data_mass.shape[0]
    own_table, mc_mass, mc_basis = call(
        prepare_kernel,
        (shape(rows, 4, LANES), shape(1, mc_count), shape(levels, mc_count, dtype=jnp.bfloat16)),
        [
            pltpu.VMEM((1, res_mass.shape[0]), jnp.float32),
            pltpu.VMEM((1, res_width.shape[0]), jnp.float32),
            pltpu.VMEM((1, res_wave.shape[0]), jnp.int32),
            pltpu.VMEM((1, OWN), jnp.int32),
            pltpu.VMEM((2, OWN), jnp.float32),
            pltpu.SemaphoreType.DMA((5,)),
            pltpu.SemaphoreType.DMA((2,)),
        ],
        res_mass[None], res_width[None], res_wave[None], wave_q[None], couplings, mc_mass[None], mc_basis,
        hbm=range(7),
    )
    table = lax.all_to_all(own_table, "wrow", 0, 0)
    tile, wide, chooser, data_mass, data_basis, weight = call(
        functools.partial(gram_kernel, 1.0 / (mc_count * events)),
        (
            shape(OWN, rows, LANES, dtype=jnp.bfloat16),
            shape(PARAMS, waves, LANES),
            shape(waves, levels, dtype=jnp.bfloat16),
            shape(1, data_count),
            shape(levels, data_count, dtype=jnp.bfloat16),
            shape(1, data_count),
        ),
        [
            pltpu.VMEM((2 * waves, TILE), jnp.bfloat16),
            pltpu.VMEM((2 * waves, LANES), jnp.float32),
            pltpu.VMEM((OWN, rows, LANES), jnp.float32),
            pltpu.SemaphoreType.DMA((3,)),
        ],
        table, mc_mass, mc_basis, data_mass[None], data_basis, data_weight[None],
        hbm=range(3, 6),
    )
    pieces = lax.all_to_all(tile, EVENT, 0, 0)
    inverse_count = 1.0 / (data_count * events)
    tile_sems = pltpu.SemaphoreType.DMA((data_count // TILE,))
    tail_shape = (2 * waves, data_count - HEAD * TILE)
    base, coupling, head, tail = call(
        functools.partial(first_kernel, inverse_count),
        (
            shape(2, LANES),
            shape(rows, LANES),
            shape(2 * waves, HEAD * TILE, dtype=jnp.bfloat16),
            pltpu.HBM(tail_shape, jnp.bfloat16),
        ),
        [pltpu.VMEM(tail_shape, jnp.bfloat16)] + pass_scratch(waves) + [tile_sems],
        table, wide, chooser, data_mass, data_basis, weight,
        hbm_out=(3,),
        cost=pl.CostEstimate(
            flops=40 * waves * data_count, bytes_accessed=8 * waves * data_count, transcendentals=waves * data_count
        ),
    )
    terms, gram_row = call(
        add_kernel, (shape(zx, 2, LANES), shape(rows, LANES)), [], pieces, base, coupling
    )

    def exchange(values):
        merged = call(merge_kernel, shape(2 * rows, 2, LANES), [], lax.all_to_all(values, ZX, 0, 0))
        return lax.all_to_all(merged, PEERS, 0, 0)

    column_scratch = [pltpu.VMEM((2, NEXT_ROWS, LANES), jnp.float32)]
    for step in range(1, ITERS):
        received = exchange(terms)
        if step == 1:
            terms, coupling, tail = call(
                functools.partial(second_kernel, inverse_count),
                (shape(zx, 2, LANES), shape(rows, LANES), shape(*tail_shape, dtype=jnp.bfloat16)),
                pass_scratch(waves) + column_scratch + [tile_sems],
                received, coupling, head, tail, weight,  gram_row,
                        hbm=(3,),
            )
        else:
            terms, coupling = call(
                functools.partial(next_kernel, inverse_count),
                (shape(zx, 2, LANES), shape(rows, LANES)),
                pass_scratch(waves) + column_scratch,
                received, coupling, head, tail, weight,  gram_row,
                    )
    received = exchange(terms)
    coupling_out, intensity = call(
        last_kernel,
        (shape(2, OWN), shape(1, data_count)),
        [
            pltpu.VMEM((8, 2 * waves), jnp.float32),
            pltpu.VMEM((rows, LANES), jnp.float32),
            pltpu.VMEM((2, LAST_ROWS, LANES), jnp.float32),
        ],
        received, coupling, head, tail,
    )
    return coupling_out, intensity.reshape(data_count)


def solution(mesh):
    chips = Mesh(mesh.devices.reshape(4, 8, 2, 8), ("z", "x", "core", "wrow"))
    placed = (
        P(EVENT),
        P(None, EVENT),
        P(EVENT),
        P(None, EVENT),
        P(EVENT),
        P("wrow"),
        P("wrow"),
        P("wrow"),
        P("wrow"),
        P(None, "wrow"),
    )
    return jax.shard_map(
        shards, mesh=chips, in_specs=placed, out_specs=(P(None, "wrow"), P(EVENT)), check_vma=False
    )
```

```python
import functools

import jax
import jax.numpy as jnp
from jax import lax
from jax.experimental import pallas as pl
from jax.experimental.pallas import tpu as pltpu
from jax.sharding import Mesh, PartitionSpec as P

ITERS = 3
BACKGROUND = 0.5
ZX = ("z", "x")
EVENT = ("z", "x", "core")
PEERS = ("core", "wrow")
OWN = 64
LANES = 128
TILE = 512
CHUNK = 16
ROWS = 8
PARAMS = 4
NEXT_ROWS = 256
LAST_ROWS = 256
HEAD = 1
VMEM_LIMIT = 24 << 20


def copies(pairs, sems):
    started = [pltpu.make_async_copy(source, target, sems.at[place]) for place, (source, target) in enumerate(pairs)]
    for copy in started:
        copy.start()
    return started


def prepare_kernel(
    mass_in, width_in, wave_in, level_in, coupling_in, mc_mass_in, mc_basis_in,
    out_ref, mc_mass_ref, mc_basis_ref, mass_ref, width_ref, wave_ref, level_ref, coupling_ref, sems, mc_sems
):
    place_ref = here()
    pairs = (
        (mass_in, mass_ref),
        (width_in, width_ref),
        (wave_in, wave_ref),
        (level_in, level_ref),
        (coupling_in, coupling_ref),
    )
    small = copies(pairs, sems)
    large = copies(((mc_mass_in, mc_mass_ref), (mc_basis_in, mc_basis_ref)), mc_sems)
    for copy in small:
        copy.wait()
    count = mass_ref.shape[1]
    local = wave_ref[...] - place_ref[0] * OWN
    index = lax.broadcasted_iota(jnp.int32, (OWN, count), 1)
    owner = lax.broadcasted_iota(jnp.int32, (OWN, count), 0) == local
    first_at = jnp.min(jnp.where(owner, index, count), axis=1, keepdims=True)
    first = owner & (index == first_at)
    second = owner & (index != first_at)
    mass = mass_ref[...]
    square = mass * mass
    inverse = 1.0 / (mass * width_ref[...])
    columns = [
        jnp.sum(jnp.where(mask, value, 0.0), axis=1, keepdims=True)
        for mask in (first, second)
        for value in (square, inverse)
    ]
    lane = lax.broadcasted_iota(jnp.int32, (OWN, LANES), 1)
    table = jnp.zeros((OWN, LANES), jnp.float32)
    for place, column in enumerate(columns):
        table = jnp.where(lane == place, column, table)
    turned = jnp.concatenate([table, jnp.zeros((LANES - OWN, LANES), jnp.float32)], axis=0).T
    rest = jnp.concatenate(
        [level_ref[...].astype(jnp.float32), coupling_ref[...], jnp.zeros((1, OWN), jnp.float32)], axis=0
    )
    rows = jnp.concatenate([turned[0:4, 0:OWN], rest], axis=1)
    send_terms(rows, out_ref)
    for copy in large:
        copy.wait()


def load_table(table_ref, wide_ref, chooser_ref):
    blocks = table_ref.shape[0]
    levels = chooser_ref.shape[1]
    stacked = [table_ref[block] for block in range(blocks)]
    stacked.append(jnp.zeros((LANES - 4 * blocks, LANES), jnp.float32))
    turned = jnp.concatenate(stacked, axis=0).T
    column = lax.broadcasted_iota(jnp.int32, (OWN, levels), 1).astype(jnp.float32)
    for block in range(blocks):
        rows = slice(block * OWN, (block + 1) * OWN)
        for pair in range(2):
            first = 4 * block + 2 * pair
            square = turned[0:OWN, first : first + 1]
            inverse = turned[0:OWN, first + 1 : first + 2]
            wide_ref[2 * pair, rows, :] = jnp.broadcast_to(square, (OWN, LANES))
            wide_ref[2 * pair + 1, rows, :] = jnp.broadcast_to(inverse, (OWN, LANES))
        level = turned[OWN : 2 * OWN, 4 * block : 4 * block + 1]
        chooser_ref[rows, :] = (level == column).astype(jnp.bfloat16)


def lineshapes(mass, wide_ref, rows):
    real = imag = None
    for pair in range(2):
        gap = (wide_ref[2 * pair, rows, :] - mass) * wide_ref[2 * pair + 1, rows, :]
        share = 1.0 / (gap * gap + 1.0)
        real = gap * share if real is None else real + gap * share
        imag = share if imag is None else imag + share
    return real, imag


def fill_tile(mass_row, basis_tile, wide_ref, chooser_ref, store):
    waves = chooser_ref.shape[0]
    masses = [
        jnp.broadcast_to(mass_row[:, half : half + LANES], (ROWS, LANES)) for half in range(0, TILE, LANES)
    ]
    for start in range(0, waves, OWN):
        angular = jnp.dot(chooser_ref[start : start + OWN, :], basis_tile, preferred_element_type=jnp.float32)
        for inner in range(0, OWN, ROWS):
            rows = slice(start + inner, start + inner + ROWS)
            reals, imags = [], []
            for half, mass in enumerate(masses):
                real, imag = lineshapes(mass, wide_ref, rows)
                scale = angular[inner : inner + ROWS, half * LANES : (half + 1) * LANES]
                reals.append(real * scale)
                imags.append(imag * scale)
            real = jnp.concatenate(reals, axis=1).astype(jnp.bfloat16)
            imag = jnp.concatenate(imags, axis=1).astype(jnp.bfloat16)
            store(2 * start + inner, real, imag)


def gram_kernel(
    scale, table_ref, mass_ref, basis_ref, data_mass_in, data_basis_in, weight_in,
    out_ref, wide_ref, chooser_ref, data_mass_ref, data_basis_ref, weight_ref,
    amp_ref, sum_ref, turn_ref, data_sems
):
    place_ref = here()
    later = copies(
        ((data_mass_in, data_mass_ref), (data_basis_in, data_basis_ref), (weight_in, weight_ref)), data_sems
    )
    load_table(table_ref, wide_ref, chooser_ref)
    sum_ref[...] = jnp.zeros_like(sum_ref)
    blocks = table_ref.shape[0]

    def store(row, real, imag):
        amp_ref[row : row + ROWS, :] = real
        amp_ref[row + OWN : row + OWN + ROWS, :] = imag

    @pl.loop(0, mass_ref.shape[1] // TILE)
    def _(step):
        columns = pl.ds(pl.multiple_of(step * TILE, TILE), TILE)
        fill_tile(mass_ref[:, columns], basis_ref[:, columns], wide_ref, chooser_ref, store)
        own = amp_ref[pl.ds(pl.multiple_of(place_ref[0] * 2 * OWN, 2 * OWN), 2 * OWN), :]
        sum_ref[...] += lax.dot_general(
            amp_ref[...], own, (((1,), (1,)), ((), ())), preferred_element_type=jnp.float32
        )

    for block in range(blocks):
        real_rows = sum_ref[2 * block * OWN : (2 * block + 1) * OWN, :]
        imag_rows = sum_ref[(2 * block + 1) * OWN : (2 * block + 2) * OWN, :]
        gram_real = real_rows + pltpu.roll(imag_rows, OWN, 1)
        gram_imag = imag_rows - pltpu.roll(real_rows, OWN, 1)
        turned = (jnp.concatenate([gram_real, gram_imag], axis=0) * scale).T
        turn_ref[:, block, :] = turned[0:OWN, :]
    out_ref[...] = turn_ref[...].astype(jnp.bfloat16)
    for copy in later:
        copy.wait()


def load_coupling(coupling, parts_ref):
    blocks = coupling.shape[0]
    signed, swapped = signs(coupling)
    parts_ref[...] = jnp.zeros_like(parts_ref)
    for row, value in enumerate((signed, swapped)):
        high = value.astype(jnp.bfloat16)
        rest = value - high.astype(jnp.float32)
        middle = rest.astype(jnp.bfloat16)
        low = (rest - middle.astype(jnp.float32)).astype(jnp.bfloat16)
        for place, part in enumerate((high, middle, low)):
            wide = part.astype(jnp.float32)
            for block in range(blocks):
                parts_ref[2 * place + row : 2 * place + row + 1, block * LANES : (block + 1) * LANES] = wide[block : block + 1]
    return signed, swapped


def load_columns(signed, swapped, vector_rows, column_ref):
    blocks = vector_rows // LANES
    first = signed.shape[0] - blocks
    rows = [signed[first:], swapped[first:], jnp.zeros((LANES - 2 * blocks, LANES), jnp.float32)]
    turned = jnp.concatenate(rows, axis=0).T
    for place in range(2):
        for block in range(blocks):
            column = turned[:, place * blocks + block : place * blocks + block + 1]
            column_ref[place, block * LANES : (block + 1) * LANES, :] = jnp.broadcast_to(column, (LANES, LANES))


def field_of(parts, amp_ref, column_ref=None):
    waves = amp_ref.shape[0]
    vector_rows = 0 if column_ref is None else column_ref.shape[1]
    matrix_rows = waves - vector_rows
    sums = jnp.dot(parts[:, :matrix_rows], amp_ref[:matrix_rows, :], preferred_element_type=jnp.float32)
    real = (sums[4:5] + sums[2:3]) + sums[0:1]
    imag = (sums[5:6] + sums[3:4]) + sums[1:2]
    if vector_rows:
        lanes = TILE // LANES
        reals = [jnp.zeros((ROWS, LANES), jnp.float32) for _ in range(lanes)]
        imags = [jnp.zeros((ROWS, LANES), jnp.float32) for _ in range(lanes)]
        for start in range(0, vector_rows, ROWS):
            rows = slice(start, start + ROWS)
            values = amp_ref[matrix_rows + start : matrix_rows + start + ROWS, :].astype(jnp.float32)
            by_real, by_imag = column_ref[0, rows, :], column_ref[1, rows, :]
            for place in range(lanes):
                value = values[:, place * LANES : (place + 1) * LANES]
                reals[place] = reals[place] + value * by_real
                imags[place] = imags[place] + value * by_imag
        real = real + jnp.sum(jnp.concatenate(reals, axis=1), axis=0, keepdims=True)
        imag = imag + jnp.sum(jnp.concatenate(imags, axis=1), axis=0, keepdims=True)
    return real, imag


def tile_at(step):
    if isinstance(step, int):
        return pl.ds(step * TILE, TILE)
    return pl.ds(pl.multiple_of(step * TILE, TILE), TILE)


def project_tile(real, imag, weight, own_tile, by_real_ref, by_imag_ref, curve_ref):
    power = real * real + imag * imag
    inverse = 1.0 / (power + BACKGROUND)
    weighting = weight * inverse
    real = real * weighting
    imag = imag * weighting
    curving = weighting * power * inverse
    for start in range(0, own_tile.shape[0], CHUNK):
        rows = slice(start, start + CHUNK)
        by_real = by_real_ref[rows, :]
        by_imag = by_imag_ref[rows, :]
        curve = curve_ref[rows, :]
        for half in range(0, own_tile.shape[1], LANES):
            lanes = slice(half, half + LANES)
            value = own_tile[rows, lanes].astype(jnp.float32)
            by_real = by_real + value * real[:, lanes]
            by_imag = by_imag + value * imag[:, lanes]
            curve = curve + value * value * curving[:, lanes]
        by_real_ref[rows, :] = by_real
        by_imag_ref[rows, :] = by_imag
        curve_ref[rows, :] = curve


def gradient_rows(scale, by_real_ref, by_imag_ref, curve_ref):
    low, high = slice(0, OWN), slice(OWN, 2 * OWN)
    grad = jnp.concatenate(
        [-(by_real_ref[low, :] + by_imag_ref[high, :]), by_real_ref[high, :] - by_imag_ref[low, :]], axis=0
    )
    curve = jnp.concatenate([curve_ref[low, :] + curve_ref[high, :], jnp.zeros((OWN, LANES), jnp.float32)], axis=0)
    grad_row = jnp.sum(grad.T, axis=0, keepdims=True) * scale
    curve_row = jnp.sum(curve.T, axis=0, keepdims=True) * scale
    return jnp.concatenate([grad_row, curve_row], axis=0)


def gram_rows(gram, signed, swapped, place_ref):
    mixed_real = jnp.sum(gram * signed, keepdims=True)
    mixed_imag = jnp.sum(gram * swapped, keepdims=True)
    row_weight = jnp.sum(jnp.abs(gram), keepdims=True)
    lane = lax.broadcasted_iota(jnp.int32, (1, LANES), 1)
    event = place_ref[1]
    grad_row = jnp.where(lane == event, mixed_real, 0.0) + jnp.where(lane == event + OWN, mixed_imag, 0.0)
    curve_row = jnp.where(lane == event + OWN, row_weight, 0.0)
    return jnp.concatenate([grad_row, curve_row], axis=0)


def signs(coupling):
    lane = lax.broadcasted_iota(jnp.int32, coupling.shape, 1)
    return jnp.where(lane < OWN, coupling, -coupling), pltpu.roll(coupling, OWN, 1)


def here():
    chip = lax.axis_index("z") * lax.axis_size("x") + lax.axis_index("x")
    return lax.axis_index("wrow"), chip * lax.axis_size("core") + lax.axis_index("core")


def send_terms(terms, out_ref):
    for peer in range(out_ref.shape[0]):
        out_ref[peer] = terms


def merge_kernel(received_ref, out_ref):
    send_terms(jnp.sum(received_ref[...], axis=0), out_ref)


def clear(*refs):
    for ref in refs:
        ref[...] = jnp.zeros_like(ref)


def own_rows(place_ref):
    return pl.ds(pl.multiple_of(place_ref[0] * 2 * OWN, 2 * OWN), 2 * OWN)


def first_kernel(
    scale, table_ref, wide_ref, chooser_ref, mass_ref, basis_ref, weight_ref,
    out_ref, coupling_ref, head_ref, amp_out, amp_ref, parts_ref, by_real_ref, by_imag_ref, curve_ref, sems
):
    place_ref = here()
    for block in range(table_ref.shape[0]):
        half = table_ref[block]
        coupling_ref[block : block + 1, :] = jnp.concatenate([half[1:2, OWN:LANES], half[2:3, OWN:LANES]], axis=1)
    load_coupling(coupling_ref[...], parts_ref)
    parts = parts_ref[...].astype(jnp.bfloat16)
    clear(by_real_ref, by_imag_ref, curve_ref)
    tail = amp_ref.shape[0]

    def compute(event_tile, target_ref):
        events = tile_at(event_tile)

        def store(row, real, imag):
            target_ref[row : row + ROWS, :] = real
            target_ref[row + OWN : row + OWN + ROWS, :] = imag

        fill_tile(mass_ref[:, events], basis_ref[:, events], wide_ref, chooser_ref, store)
        real, imag = field_of(parts, target_ref)
        own = target_ref[own_rows(place_ref), :]
        project_tile(real, imag, weight_ref[:, events], own, by_real_ref, by_imag_ref, curve_ref)

    def copy(step):
        return pltpu.make_async_copy(amp_ref.at[step], amp_out.at[step], sems.at[step])

    @pl.loop(0, tail)
    def _(step):
        compute(step + HEAD, amp_ref.at[step])
        copy(step).start()

    compute(0, head_ref)
    out_ref[...] = gradient_rows(scale, by_real_ref, by_imag_ref, curve_ref)
    for step in range(tail):
        copy(step).wait()


def add_kernel(pieces_ref, base_ref, coupling_ref, out_ref, gram_ref):
    place_ref = here()
    gram = jnp.sum(pieces_ref[...].astype(jnp.float32), axis=0)
    gram_ref[...] = gram
    send_terms(base_ref[...] + gram_rows(gram, *signs(coupling_ref[...]), place_ref), out_ref)


def new_coupling(received_ref, coupling_ref):
    blocks = coupling_ref.shape[0]
    total = received_ref[0:blocks] + received_ref[blocks : 2 * blocks]
    grad = total[:, 0, :]
    curve = total[:, 1, :]
    return coupling_ref[...] - grad / (curve + pltpu.roll(curve, OWN, 1))


def next_pass(
    scale, received_ref, old_ref, head_ref, tail_ref, arrive, weight_ref, gram_ref, out_ref, coupling_ref,
    parts_ref, by_real_ref, by_imag_ref, curve_ref, column_ref
):
    place_ref = here()
    coupling = new_coupling(received_ref, old_ref)
    coupling_ref[...] = coupling
    signed, swapped = load_coupling(coupling, parts_ref)
    load_columns(signed, swapped, column_ref.shape[1], column_ref)
    parts = parts_ref[...].astype(jnp.bfloat16)
    clear(by_real_ref, by_imag_ref, curve_ref)
    tiles = tail_ref.shape[0]

    def field_at(source_ref):
        return field_of(parts, source_ref, column_ref)

    def project(source_ref, event_tile, field):
        own = source_ref[own_rows(place_ref), :]
        project_tile(*field, weight_ref[:, tile_at(event_tile)], own, by_real_ref, by_imag_ref, curve_ref)

    def ahead(step, field):
        arrive(step + 1)
        later = field_at(tail_ref.at[step + 1])
        project(tail_ref.at[step], step + HEAD, field)
        return later

    field = field_at(head_ref)
    arrive(0)
    later = field_at(tail_ref.at[0])
    project(head_ref, 0, field)
    field = lax.fori_loop(0, tiles - 1, ahead, later)
    project(tail_ref.at[tiles - 1], tiles - 1 + HEAD, field)
    terms = gradient_rows(scale, by_real_ref, by_imag_ref, curve_ref)
    send_terms(terms + gram_rows(gram_ref[...], signed, swapped, place_ref), out_ref)


def second_kernel(
    scale, received_ref, old_ref, head_ref, tail_in, weight_ref, gram_ref, out_ref, coupling_ref, tail_ref, *scratch
):
    sems = scratch[-1]

    def copy(step):
        return pltpu.make_async_copy(tail_in.at[step], tail_ref.at[step], sems.at[step])

    for step in range(tail_ref.shape[0]):
        copy(step).start()
    next_pass(
        scale, received_ref, old_ref, head_ref, tail_ref, lambda step: copy(step).wait(), weight_ref, gram_ref,
        out_ref, coupling_ref, *scratch[:-1]
    )


def next_kernel(scale, received_ref, old_ref, head_ref, tail_ref, *rest):
    next_pass(scale, received_ref, old_ref, head_ref, tail_ref, lambda step: None, *rest)


def last_kernel(
    received_ref, old_ref, head_ref, tail_ref, coupling_out_ref, intensity_ref, parts_ref, coupling_ref, column_ref
):
    place_ref = here()
    coupling = new_coupling(received_ref, old_ref)
    coupling_ref[...] = coupling
    signed, swapped = load_coupling(coupling, parts_ref)
    load_columns(signed, swapped, column_ref.shape[1], column_ref)
    parts = parts_ref[...].astype(jnp.bfloat16)
    mine = coupling_ref[pl.ds(place_ref[0], 1), :]
    coupling_out_ref[0:1, :] = mine[:, 0:OWN]
    coupling_out_ref[1:2, :] = pltpu.roll(mine, OWN, 1)[:, 0:OWN]

    def finish(source_ref, event_tile):
        real, imag = field_of(parts, source_ref, column_ref)
        intensity_ref[:, tile_at(event_tile)] = real * real + imag * imag + BACKGROUND

    finish(head_ref, 0)

    @pl.loop(0, tail_ref.shape[0])
    def _(step):
        finish(tail_ref.at[step], step + HEAD)


def call(kernel, outs, scratch, *args, hbm=(), hbm_out=(), cost=None):
    def space(place):
        return pltpu.HBM if place in hbm else pltpu.VMEM

    single = not isinstance(outs, tuple)
    whole = pl.BlockSpec(memory_space=pltpu.VMEM)
    return pl.pallas_call(
        kernel,
        out_shape=outs,
        in_specs=[pl.BlockSpec(memory_space=space(place)) for place in range(len(args))],
        out_specs=whole
        if single
        else tuple(pl.BlockSpec(memory_space=pltpu.HBM) if place in hbm_out else whole for place in range(len(outs))),
        cost_estimate=cost,
        scratch_shapes=scratch,
        compiler_params=pltpu.CompilerParams(vmem_limit_bytes=VMEM_LIMIT),
    )(*(pltpu.with_memory_space_constraint(arg, pltpu.HBM) if place in hbm else arg for place, arg in enumerate(args)))


def shape(*dims, dtype=jnp.float32):
    return jax.ShapeDtypeStruct(dims, dtype)


def pass_scratch(waves):
    return [pltpu.VMEM((8, 2 * waves), jnp.float32)] + [pltpu.VMEM((2 * OWN, LANES), jnp.float32) for _ in range(3)]


def shards(
    mc_mass, mc_basis, data_mass, data_basis, data_weight, res_mass, res_width, res_wave, wave_q, couplings
):
    rows = lax.axis_size("wrow")
    waves = OWN * rows
    zx = lax.axis_size("z") * lax.axis_size("x")
    events = zx * lax.axis_size("core")
    levels = mc_basis.shape[0]
    mc_count, data_count = mc_mass.shape[0], data_mass.shape[0]
    own_table, mc_mass, mc_basis = call(
        prepare_kernel,
        (shape(rows, 4, LANES), shape(1, mc_count), shape(levels, mc_count, dtype=jnp.bfloat16)),
        [
            pltpu.VMEM((1, res_mass.shape[0]), jnp.float32),
            pltpu.VMEM((1, res_width.shape[0]), jnp.float32),
            pltpu.VMEM((1, res_wave.shape[0]), jnp.int32),
            pltpu.VMEM((1, OWN), jnp.int32),
            pltpu.VMEM((2, OWN), jnp.float32),
            pltpu.SemaphoreType.DMA((5,)),
            pltpu.SemaphoreType.DMA((2,)),
        ],
        res_mass[None], res_width[None], res_wave[None], wave_q[None], couplings, mc_mass[None], mc_basis,
        hbm=range(7),
    )
    table = lax.all_to_all(own_table, "wrow", 0, 0)
    tile, wide, chooser, data_mass, data_basis, weight = call(
        functools.partial(gram_kernel, 1.0 / (mc_count * events)),
        (
            shape(OWN, rows, LANES, dtype=jnp.bfloat16),
            shape(PARAMS, waves, LANES),
            shape(waves, levels, dtype=jnp.bfloat16),
            shape(1, data_count),
            shape(levels, data_count, dtype=jnp.bfloat16),
            shape(1, data_count),
        ),
        [
            pltpu.VMEM((2 * waves, TILE), jnp.bfloat16),
            pltpu.VMEM((2 * waves, LANES), jnp.float32),
            pltpu.VMEM((OWN, rows, LANES), jnp.float32),
            pltpu.SemaphoreType.DMA((3,)),
        ],
        table, mc_mass, mc_basis, data_mass[None], data_basis, data_weight[None],
        hbm=range(3, 6),
    )
    pieces = lax.all_to_all(tile, EVENT, 0, 0)
    inverse_count = 1.0 / (data_count * events)
    tile_sems = pltpu.SemaphoreType.DMA((data_count // TILE,))
    tail_shape = (data_count // TILE - HEAD, 2 * waves, TILE)
    base, coupling, head, tail = call(
        functools.partial(first_kernel, inverse_count),
        (
            shape(2, LANES),
            shape(rows, LANES),
            shape(2 * waves, HEAD * TILE, dtype=jnp.bfloat16),
            pltpu.HBM(tail_shape, jnp.bfloat16),
        ),
        [pltpu.VMEM(tail_shape, jnp.bfloat16)] + pass_scratch(waves) + [tile_sems],
        table, wide, chooser, data_mass, data_basis, weight,
        hbm_out=(3,),
        cost=pl.CostEstimate(
            flops=40 * waves * data_count, bytes_accessed=8 * waves * data_count, transcendentals=waves * data_count
        ),
    )
    terms, gram_row = call(
        add_kernel, (shape(zx, 2, LANES), shape(rows, LANES)), [], pieces, base, coupling
    )

    def exchange(values):
        merged = call(merge_kernel, shape(2 * rows, 2, LANES), [], lax.all_to_all(values, ZX, 0, 0))
        return lax.all_to_all(merged, PEERS, 0, 0)

    column_scratch = [pltpu.VMEM((2, NEXT_ROWS, LANES), jnp.float32)]
    for step in range(1, ITERS):
        received = exchange(terms)
        if step == 1:
            terms, coupling, tail = call(
                functools.partial(second_kernel, inverse_count),
                (shape(zx, 2, LANES), shape(rows, LANES), shape(*tail_shape, dtype=jnp.bfloat16)),
                pass_scratch(waves) + column_scratch + [tile_sems],
                received, coupling, head, tail, weight,  gram_row,
                        hbm=(3,),
            )
        else:
            terms, coupling = call(
                functools.partial(next_kernel, inverse_count),
                (shape(zx, 2, LANES), shape(rows, LANES)),
                pass_scratch(waves) + column_scratch,
                received, coupling, head, tail, weight,  gram_row,
                    )
    received = exchange(terms)
    coupling_out, intensity = call(
        last_kernel,
        (shape(2, OWN), shape(1, data_count)),
        [
            pltpu.VMEM((8, 2 * waves), jnp.float32),
            pltpu.VMEM((rows, LANES), jnp.float32),
            pltpu.VMEM((2, LAST_ROWS, LANES), jnp.float32),
        ],
        received, coupling, head, tail,
    )
    return coupling_out, intensity.reshape(data_count)


def solution(mesh):
    chips = Mesh(mesh.devices.reshape(4, 8, 2, 8), ("z", "x", "core", "wrow"))
    placed = (
        P(EVENT),
        P(None, EVENT),
        P(EVENT),
        P(None, EVENT),
        P(EVENT),
        P("wrow"),
        P("wrow"),
        P("wrow"),
        P("wrow"),
        P(None, "wrow"),
    )
    return jax.shard_map(
        shards, mesh=chips, in_specs=placed, out_specs=(P(None, "wrow"), P(EVENT)), check_vma=False
    )
```
